256 devices in a mesh: bevy: 16 (over y, x), bevx: 8 (over z), cam: 2 (over core).
Axes of the slice: x: 4, y: 4, z: 8, core: 2. Of those that a mesh axis runs over, the one named last changes fastest.
Arguments:
- image_tokens: bfloat16 [65536, 768], P(('bevy', 'bevx', 'cam')), may hold values from -6 to 6
- lift_weight: bfloat16 [768, 1024], replicated, may hold values from -0.21875 to 0.21875
- route_token: int32 [128, 2, 128, 8], P(('bevy', 'bevx'), 'cam'), may hold values from 0 to 255
- route_cell: int32 [128, 2, 128, 8], P(None, 'cam', ('bevy', 'bevx')), may hold values from 0 to 1023
- slot_counts: int32 [128, 2, 128], P(('bevy', 'bevx'), 'cam'), may hold values from 0 to 8, as said below
- norm_gain: float32 [1024], replicated, may hold values from 0.1 to 1.9
- w_query: bfloat16 [1024, 1024], replicated, may hold values from -0.1875 to 0.1875
- w_key: bfloat16 [1024, 1024], replicated, may hold values from -0.1875 to 0.1875
- w_value: bfloat16 [1024, 1024], replicated, may hold values from -0.1875 to 0.1875
- w_out: bfloat16 [1024, 1024], replicated, may hold values from -0.1875 to 0.1875
- key_bias: bfloat16 [256, 512, 16], P(None, 'bevx'), may hold values from -1.5 to 260
Outputs:
- bev_out: bfloat16 [256, 512, 1024], P(('bevy', 'cam'), 'bevx')
The draws below stay inside these ranges and needn't reach their ends.
Inputs may be any that keep to these rules, and one draw needn't show every extreme that they name: The first slot_counts slots of a source device and tile are live; at most 8. In every draw some tile receives 8 live slots from every source device.
All inputs are finite; a program needn't handle non-finite values.
Results may differ from the reference program's by a relative error of at most 0.0055.
Values may be sent and summed in bfloat16 or wider, within the bound.
No kernel may reach another device: no remote copies, remote signals or barrier semaphores. Data moves between devices by JAX's collectives and lax.ppermute only.
A program may use at most 128 MiB of HBM per device.

```python
import jax
import jax.numpy as jnp
from jax import lax

IN_W = 768
D = 1024
HEADS = 16
HEAD_DIM = 64
TOK_DEV = 256
SLOT = 8
ROWS_DEV = 8
COLS_DEV = 64
HALO = 4
TILES = 128
CELLS = 1024
GRID_R = 256
GRID_C = 512
TOKENS = 65536
N_BEVY = 16
N_BEVX = 8
N_CAM = 2


def draw_slot_counts(key, part):
    first, second, third, fourth = jax.random.split(key, 4)
    shape_all = (TILES, N_CAM, TILES)
    ceiling = jax.random.randint(first, (1, 1, TILES), SLOT // 4, SLOT + 1)
    base_counts = jnp.minimum(jax.random.randint(second, shape_all, 0, SLOT + 1), ceiling)
    hot_source = jax.random.randint(third, (TILES, N_CAM, 1), 0, TILES)
    hot_tile = jax.random.randint(fourth, (), 0, TILES)
    tile_ids = lax.broadcasted_iota(jnp.int32, shape_all, 2)
    filled = (tile_ids == hot_source) | (tile_ids == hot_tile)
    return jnp.where(filled, SLOT, base_counts).astype(jnp.int32)


def peak_mask(row_key, col_key, on_key):
    block_rows = GRID_R // ROWS_DEV
    block_cols = GRID_C // COLS_DEV
    block_shape = (block_rows, 1, block_cols, 1, HEADS)
    full_shape = (block_rows, ROWS_DEV, block_cols, COLS_DEV, HEADS)
    peak_row = jax.random.randint(row_key, block_shape, 0, ROWS_DEV)
    peak_col = jax.random.randint(col_key, block_shape, 0, COLS_DEV)
    peak_on = jax.random.bernoulli(on_key, 0.5, block_shape)
    row_inside = lax.broadcasted_iota(jnp.int32, full_shape, 1)
    col_inside = lax.broadcasted_iota(jnp.int32, full_shape, 3)
    chosen = peak_on & (row_inside == peak_row) & (col_inside == peak_col)
    return chosen.reshape(GRID_R, GRID_C, HEADS)


def draw_key_bias(key, part):
    first, second, third, fourth = jax.random.split(key, 4)
    shape_all = (GRID_R, GRID_C, HEADS)
    peaks = peak_mask(second, third, fourth)
    flat_bias = jax.random.uniform(first, shape_all, jnp.float32, -1.0, 1.0)
    return jnp.where(peaks, 6.0, flat_bias).astype(jnp.bfloat16)


def set_ends(values, rng, least, largest):
    place = [jax.random.randint(jax.random.fold_in(rng, axis), (), 0, length) for axis, length in enumerate(values.shape)]
    longest = values.shape.index(max(values.shape))
    neighbour = place[:longest] + [(place[longest] + 1) % values.shape[longest]] + place[longest + 1:]
    return values.at[tuple(place)].set(least).at[tuple(neighbour)].set(largest)


def block_scale(own_key, shape, cuts, low, top_value):
    gain, own = 1.0, jax.random.fold_in(own_key, 6)
    for dim, parts in cuts:
        heights = jnp.exp(jax.random.uniform(jax.random.fold_in(own, dim), (parts,), jnp.float32, low / len(cuts), top_value / len(cuts)))
        gain = gain * jnp.repeat(heights, shape[dim] // parts).reshape([-1 if axis == dim else 1 for axis in range(len(shape))])
    return gain


def scatter_about(rng, shape, width, reach, cuts=(), kind=jnp.bfloat16):
    gain = block_scale(rng, shape, cuts, -0.22, 0.18) if cuts else 1.0
    entries = jax.random.normal(rng, shape, jnp.float32) * width * gain
    return jnp.minimum(jnp.maximum(entries, -reach), reach).astype(kind)


def setup_inputs(seed: int = 0) -> dict:
    seeds = jax.random.split(jax.random.key(seed), 12)
    return {
        "image_tokens": scatter_about(seeds[0], (TOKENS, IN_W), 1.0, 6.0, ((0, 256),)),
        "lift_weight": scatter_about(seeds[1], (IN_W, D), IN_W ** -0.5, 0.21875),
        "route_token": set_ends(jax.random.randint(seeds[2], (TILES, N_CAM, TILES, SLOT), 0, TOK_DEV), jax.random.fold_in(seeds[2], 1), 0, TOK_DEV - 1).astype(jnp.int32),
        "route_cell": set_ends(jax.random.randint(seeds[3], (TILES, N_CAM, TILES, SLOT), 0, CELLS), jax.random.fold_in(seeds[3], 1), 0, CELLS - 1).astype(jnp.int32),
        "slot_counts": draw_slot_counts(jax.random.fold_in(seeds[11], 71), 0),
        "norm_gain": jnp.clip(1.0 + 0.18 * jax.random.normal(seeds[5], (D,), jnp.float32), 0.1, 1.9),
        "w_query": scatter_about(seeds[6], (D, D), D ** -0.5, 0.1875),
        "w_key": scatter_about(seeds[7], (D, D), D ** -0.5, 0.1875),
        "w_value": scatter_about(seeds[8], (D, D), D ** -0.5, 0.1875),
        "w_out": scatter_about(seeds[9], (D, D), D ** -0.5, 0.1875),
        "key_bias": draw_key_bias(jax.random.fold_in(seeds[11], 71), 0),
    }


def reference(image_tokens, lift_weight, route_token, route_cell, slot_counts, norm_gain, w_query, w_key, w_value, w_out, key_bias):
    tile_count = N_BEVY * N_BEVX
    projected = jnp.dot(image_tokens, lift_weight, preferred_element_type=jnp.float32).astype(jnp.bfloat16)
    source_base = (jnp.arange(tile_count, dtype=jnp.int32)[:, None] * N_CAM + jnp.arange(N_CAM, dtype=jnp.int32)[None, :]) * TOK_DEV
    global_index = (source_base[:, :, None, None] + route_token).astype(jnp.int32)
    is_live = jnp.arange(SLOT, dtype=jnp.int32)[None, None, None, :] < slot_counts[..., None]

    def lift_tile(tile_index):
        token_ids = global_index[:, :, tile_index, :].reshape(-1)
        live_now = is_live[:, :, tile_index, :].reshape(-1)
        cell_index = route_cell[:, :, tile_index, :].reshape(-1)
        slot_rows = jnp.where(live_now[:, None], projected[token_ids].astype(jnp.float32), jnp.float32(0.0))
        return jax.ops.segment_sum(slot_rows, cell_index, num_segments=CELLS)
    tile_sums = lax.map(lift_tile, jnp.arange(tile_count, dtype=jnp.int32))
    lifted = tile_sums.reshape(N_BEVY, N_BEVX, N_CAM * ROWS_DEV, COLS_DEV, D)
    lifted = lifted.transpose(0, 2, 1, 3, 4).reshape(GRID_R, GRID_C, D)
    mean_square = lax.optimization_barrier(jnp.mean(lifted * lifted, axis=-1, keepdims=True))
    normed = (lifted * lax.rsqrt(mean_square + 1e-06) * norm_gain).astype(jnp.bfloat16)
    flat_normed = normed.reshape(-1, D)
    queries = jnp.dot(flat_normed, w_query, preferred_element_type=jnp.float32).astype(jnp.bfloat16).reshape(GRID_R, GRID_C, D)
    key_vectors = jnp.dot(flat_normed, w_key, preferred_element_type=jnp.float32).astype(jnp.bfloat16).reshape(GRID_R, GRID_C, D)
    value_vectors = jnp.dot(flat_normed, w_value, preferred_element_type=jnp.float32).astype(jnp.bfloat16).reshape(GRID_R, GRID_C, D)
    pad_rows = ((HALO, HALO), (0, 0), (0, 0))
    key_padded = jnp.pad(key_vectors, pad_rows)
    value_padded = jnp.pad(value_vectors, pad_rows)
    bias_padded = jnp.pad(key_bias, pad_rows)
    window_count = GRID_C // COLS_DEV
    block_count = GRID_R // ROWS_DEV
    score_scale = HEAD_DIM ** (-0.5)

    def window_block(block_index):
        first_row = (block_index * ROWS_DEV).astype(jnp.int32)
        query_block = lax.dynamic_slice_in_dim(queries, first_row, ROWS_DEV, 0)
        key_block = lax.dynamic_slice_in_dim(key_padded, first_row, 2 * ROWS_DEV, 0)
        value_block = lax.dynamic_slice_in_dim(value_padded, first_row, 2 * ROWS_DEV, 0)
        bias_block = lax.dynamic_slice_in_dim(bias_padded, first_row, 2 * ROWS_DEV, 0)
        query_win = query_block.reshape(ROWS_DEV, window_count, COLS_DEV, HEADS, HEAD_DIM).transpose(1, 0, 2, 3, 4).reshape(window_count, ROWS_DEV * COLS_DEV, HEADS, HEAD_DIM)
        key_win = key_block.reshape(2 * ROWS_DEV, window_count, COLS_DEV, HEADS, HEAD_DIM).transpose(1, 0, 2, 3, 4).reshape(window_count, 2 * ROWS_DEV * COLS_DEV, HEADS, HEAD_DIM)
        value_win = value_block.reshape(2 * ROWS_DEV, window_count, COLS_DEV, HEADS, HEAD_DIM).transpose(1, 0, 2, 3, 4).reshape(window_count, 2 * ROWS_DEV * COLS_DEV, HEADS, HEAD_DIM)
        bias_win = bias_block.reshape(2 * ROWS_DEV, window_count, COLS_DEV, HEADS).transpose(1, 0, 2, 3).reshape(window_count, 2 * ROWS_DEV * COLS_DEV, HEADS)
        key_row = first_row - HALO + jnp.arange(2 * ROWS_DEV, dtype=jnp.int32)
        key_valid = jnp.repeat((key_row >= 0) & (key_row < GRID_R), COLS_DEV)
        scores = jnp.einsum('wqhd,wkhd->whqk', query_win.astype(jnp.float32), key_win.astype(jnp.float32)) * score_scale
        scores = scores + bias_win.astype(jnp.float32).transpose(0, 2, 1)[:, :, None, :]
        scores = jnp.where(key_valid[None, None, None, :], scores, -jnp.inf)
        top_score = lax.optimization_barrier(jnp.max(scores, axis=-1, keepdims=True))
        expo = jnp.exp(scores - top_score)
        weights = (expo / lax.optimization_barrier(jnp.sum(expo, axis=-1, keepdims=True))).astype(jnp.bfloat16)
        attended = jnp.einsum('whqk,wkhd->wqhd', weights.astype(jnp.float32), value_win.astype(jnp.float32)).astype(jnp.bfloat16)
        return attended.reshape(window_count, ROWS_DEV, COLS_DEV, D).transpose(1, 0, 2, 3).reshape(ROWS_DEV, GRID_C, D)
    attended = lax.map(window_block, jnp.arange(block_count, dtype=jnp.int32)).reshape(GRID_R * GRID_C, D)
    mixed = jnp.dot(attended, w_out, preferred_element_type=jnp.float32).reshape(GRID_R, GRID_C, D)
    return (lifted + mixed).astype(jnp.bfloat16)
```

```python
import jax
import jax.numpy as jnp
from jax import lax
from jax.experimental import pallas as pl
from jax.experimental.pallas import tpu as pltpu
from jax.sharding import PartitionSpec as P


ROWS_DEV = 8
COLS_DEV = 64
HALO = 4
MASKED = -1e30
EARLY = (0, -1, 1, -2, 2)
LATE = (-3, 3, 4)


def whole(x):
    return pl.BlockSpec(x.shape, lambda *_: (0,) * x.ndim)


SCALAR = pl.BlockSpec(memory_space=pltpu.SMEM)
LOCAL = pl.BlockSpec(memory_space=pltpu.VMEM)


def pick_kernel(offsets, n_x, at_ref, route_ref, *refs):
    blocks, out_ref = refs[:-1], refs[-1]
    used = 0
    for i, offset in enumerate(offsets):
        parts = 2 if offset == n_x // 2 else 1
        line = (at_ref[0] + (offset + n_x)) % n_x
        index = route_ref[pl.ds(line, 1), :]
        base = 0
        rows = None
        for block in blocks[used : used + parts]:
            ids = lax.broadcasted_iota(jnp.int32, (block.shape[0], index.shape[1]), 0) + base
            one_hot = jnp.where(ids == index, 1.0, 0.0).astype(jnp.bfloat16)
            got = lax.dot_general(
                one_hot,
                block[...],
                (((0,), (0,)), ((), ())),
                preferred_element_type=jnp.float32,
            )
            rows = got if rows is None else rows + got
            base += block.shape[0]
        used += parts
        out_ref[:, i] = rows.reshape(out_ref.shape[0], out_ref.shape[2], out_ref.shape[3]).astype(
            jnp.bfloat16
        )


def pick(offsets, n_x, n_y, at, route, blocks):
    slots = route.shape[1] // n_y
    width = blocks[0].shape[1]
    return pl.pallas_call(
        lambda *refs: pick_kernel(offsets, n_x, *refs),
        in_specs=[SCALAR] + [LOCAL] * (1 + len(blocks)),
        out_specs=LOCAL,
        out_shape=jax.ShapeDtypeStruct((n_y, len(offsets), slots, width), jnp.bfloat16),
        name="pick_rows",
    )(at, route, *blocks)


def summed(offsets, n_x, at_ref, pairs, w_ref, total):
    for rows_ref, cell_ref in pairs:
        pieces = []
        hots = []
        for i, offset in enumerate(offsets):
            line = (at_ref[0] + (offset + n_x)) % n_x
            cell = cell_ref[pl.ds(line, 1), :]
            piece = rows_ref[:, i]
            pieces.append(piece.reshape(-1, piece.shape[-1]))
            ids = lax.broadcasted_iota(jnp.int32, (total.shape[0], cell.shape[1]), 0) + at_ref[1]
            hots.append(jnp.where(ids == cell, 1.0, 0.0).astype(jnp.bfloat16))
        projected = jnp.dot(
            jnp.concatenate(pieces, axis=0), w_ref[...], preferred_element_type=jnp.float32
        ).astype(jnp.bfloat16)
        total[...] += jnp.dot(
            jnp.concatenate(hots, axis=1), projected, preferred_element_type=jnp.float32
        )


def first_sum_kernel(n_x, at_ref, a_ref, ac_ref, b_ref, bc_ref, w_ref, out_ref):
    out_ref[...] = jnp.zeros_like(out_ref)
    summed(EARLY, n_x, at_ref, ((a_ref, ac_ref), (b_ref, bc_ref)), w_ref, out_ref)


def next_sum_kernel(n_x, at_ref, total_ref, a_ref, ac_ref, w_ref, out_ref):
    out_ref[...] = total_ref[...]
    summed(LATE, n_x, at_ref, ((a_ref, ac_ref),), w_ref, out_ref)


def last_sum_kernel(
    n_x, edge, at_ref, total_ref, a_ref, ac_ref, w_ref, gain_ref, own_ref, normed_ref, sent_ref, acc
):
    acc[...] = total_ref[...]
    summed(LATE, n_x, at_ref, ((a_ref, ac_ref),), w_ref, acc)
    rows = own_ref.shape[0]
    own_ref[...] = acc[pl.ds(pl.multiple_of(at_ref[1], edge), rows), :]
    for start in range(0, acc.shape[0], edge):
        lifted = acc[start : start + edge]
        mean_square = jnp.mean(lifted * lifted, axis=-1, keepdims=True)
        normed_ref[start : start + edge] = (
            lifted * lax.rsqrt(mean_square + 1e-06) * gain_ref[...]
        ).astype(jnp.bfloat16)
    sent_ref[...] = normed_ref[pl.ds(pl.multiple_of(2 * at_ref[1], edge), edge), :]


def local_call(kernel, operands, outs, scratch=()):
    return pl.pallas_call(
        kernel,
        in_specs=[SCALAR] + [LOCAL] * (len(operands) - 1),
        out_specs=[LOCAL] * len(outs),
        out_shape=outs,
        scratch_shapes=scratch,
    )(*operands)


def project_kernel(at_ref, x_ref, wq_ref, wk_ref, wv_ref, q_ref, k_ref, v_ref):
    rows = q_ref.shape[0]
    own = x_ref[pl.ds(pl.multiple_of(at_ref[1], rows // 2), rows), :]
    x = x_ref[...]
    q_ref[...] = (jnp.dot(own, wq_ref[...], preferred_element_type=jnp.float32)).astype(
        jnp.bfloat16
    )
    k_ref[...] = jnp.dot(x, wk_ref[...], preferred_element_type=jnp.float32).astype(jnp.bfloat16)
    v_ref[...] = jnp.dot(x, wv_ref[...], preferred_element_type=jnp.float32).astype(jnp.bfloat16)


def project(at, x, w_query, w_key, w_value, rows):
    ext, width = x.shape
    block = 256
    column = lambda r: pl.BlockSpec((r, block), lambda i: (0, i))
    return pl.pallas_call(
        project_kernel,
        grid=(width // block,),
        in_specs=[SCALAR, whole(x)] + [column(width)] * 3,
        out_specs=[column(rows), column(ext), column(ext)],
        out_shape=[
            jax.ShapeDtypeStruct((r, width), jnp.bfloat16) for r in (rows, ext, ext)
        ],
        compiler_params=pltpu.CompilerParams(dimension_semantics=("arbitrary",)),
        name="near_projections",
    )(at, x, w_query, w_key, w_value)


def attention_kernel(
    q_ref, k_ref, v_ref, far_ref, wk_ref, wv_ref, bias_ref, wo_ref, lifted_ref, out_ref, att_ref
):
    step = pl.program_id(0)
    rows_q = q_ref.shape[0]
    chunk = 256
    far = far_ref[...]
    far_k = jnp.dot(far, wk_ref[...], preferred_element_type=jnp.float32).astype(jnp.bfloat16)
    far_v = jnp.dot(far, wv_ref[...], preferred_element_type=jnp.float32).astype(jnp.bfloat16)
    lane = lax.broadcasted_iota(jnp.int32, (chunk, 128), 1)
    for pair in range(2):
        cut = slice(pair * 128, pair * 128 + 128)
        k = jnp.concatenate([k_ref[:, cut], far_k[:, cut]], axis=0)
        v = jnp.concatenate([v_ref[:, cut], far_v[:, cut]], axis=0)
        keys = jnp.concatenate([k, bias_ref[...]], axis=1)
        values = jnp.concatenate([v, jnp.ones_like(v)], axis=1)
        for start in range(0, rows_q, chunk):
            q = q_ref[start : start + chunk, cut] * jnp.asarray(0.125, jnp.bfloat16)
            done = []
            for side in range(2):
                own = (lane >= 64) if side else (lane < 64)
                query = jnp.concatenate(
                    [
                        jnp.where(own, q, jnp.zeros((), jnp.bfloat16)),
                        jnp.where(lane == 4 * step + 2 * pair + side, 1.0, 0.0).astype(
                            jnp.bfloat16
                        ),
                    ],
                    axis=1,
                )
                score = lax.dot_general(
                    query, keys, (((1,), (1,)), ((), ())), preferred_element_type=jnp.float32
                )
                top = jnp.max(score, axis=1, keepdims=True)
                weight = jnp.exp(score - top).astype(jnp.bfloat16)
                total = jnp.dot(weight, values, preferred_element_type=jnp.float32)
                done.append(total[:, :128] / total[:, 128:])
            att_ref[2 * step + pair, start : start + chunk] = jnp.where(
                lane < 64, done[0], done[1]
            ).astype(jnp.bfloat16)

    @pl.when(step == pl.num_programs(0) - 1)
    def _():
        attended = jnp.concatenate([att_ref[i] for i in range(att_ref.shape[0])], axis=1)
        mixed = jnp.dot(attended, wo_ref[...], preferred_element_type=jnp.float32)
        out_ref[...] = (lifted_ref[...] + mixed).astype(jnp.bfloat16)


def attention(q, k, v, far, w_key, w_value, bias, w_out, lifted):
    rows, width = q.shape
    block = 256
    column = lambda x: pl.BlockSpec((x.shape[0], block), lambda i: (0, i))
    return pl.pallas_call(
        attention_kernel,
        grid=(width // block,),
        in_specs=[
            column(q),
            column(k),
            column(v),
            whole(far),
            column(w_key),
            column(w_value),
            whole(bias),
            whole(w_out),
            whole(lifted),
        ],
        out_specs=pl.BlockSpec((rows, width), lambda i: (0, 0)),
        out_shape=jax.ShapeDtypeStruct((rows, width), jnp.bfloat16),
        scratch_shapes=[pltpu.VMEM((width // 128, rows, 128), jnp.bfloat16)],
        compiler_params=pltpu.CompilerParams(dimension_semantics=("arbitrary",)),
        name="window_attention",
    )(q, k, v, far, w_key, w_value, bias, w_out, lifted)


def steps(
    image_tokens,
    lift_weight,
    route_token,
    route_cell,
    slot_counts,
    norm_gain,
    w_query,
    w_key,
    w_value,
    w_out,
    key_bias,
):
    n_y = lax.axis_size("bevy")
    n_x = lax.axis_size("bevx")
    slot_count = route_token.shape[3]
    tokens = image_tokens.shape[0]
    width = lift_weight.shape[1]
    head_count = key_bias.shape[2]
    grid_rows = key_bias.shape[0]
    own_cells = ROWS_DEV * COLS_DEV
    edge = HALO * COLS_DEV
    ext = own_cells + edge
    row = lax.axis_index("bevy")
    col = lax.axis_index("bevx")
    core = lax.axis_index("cam")
    up = [(i, (i + 1) % n_x) for i in range(n_x)]
    down = [(b, a) for a, b in up]
    swap = [(0, 1), (1, 0)]
    at = jnp.stack([col, core * edge]).astype(jnp.int32)

    def shift(value, perm):
        return lax.ppermute(value, "bevx", perm)

    u1 = shift(image_tokens, up)
    d1 = shift(image_tokens, down)

    def by_column(value):
        return value.reshape(n_y, n_x, slot_count).transpose(1, 0, 2).reshape(n_x, -1)

    is_live = (
        lax.broadcasted_iota(jnp.int32, route_token.shape[2:], 1) < slot_counts[0, 0][:, None]
    )
    route = by_column(jnp.where(is_live, route_token[0, 0], -1))
    cells = by_column(route_cell[:, 0, 0, :])
    route, cells = lax.optimization_barrier((route, cells))
    cells_other = lax.ppermute(cells, "cam", swap)
    route = lax.all_to_all(route, "bevx", split_axis=0, concat_axis=0, tiled=True)

    u2 = shift(u1, up)
    d2 = shift(d1, down)
    u3 = shift(u2, up)
    d3 = shift(d2, down)
    half = tokens // 2
    u4 = shift(u3[:half], up)
    d4 = shift(d3[half:], down)

    near_row = (row * 2 + core) * ROWS_DEV - core * HALO
    far_row = (row * 2 + core) * ROWS_DEV + jnp.where(core == 0, -HALO, ROWS_DEV)
    far_ok = (far_row >= 0) & (far_row < grid_rows)
    near_bias = lax.dynamic_slice_in_dim(key_bias, near_row, ROWS_DEV + HALO, 0)
    far_bias = lax.dynamic_slice_in_dim(
        key_bias, jnp.clip(far_row, 0, grid_rows - HALO), HALO, 0
    )
    far_bias = jnp.where(far_ok, far_bias, jnp.asarray(MASKED, jnp.bfloat16))
    bias = jnp.concatenate([near_bias, far_bias], axis=0).reshape(-1, head_count)
    bias = jnp.pad(bias, ((0, 0), (0, 128 - head_count)))

    def exchange(rows):
        got = lax.all_to_all(rows, "bevy", split_axis=0, concat_axis=0, tiled=True)
        return got, lax.ppermute(got, "cam", swap)

    rows = pick(EARLY, n_x, n_y, at, route, (image_tokens, u1, d1, u2, d2))
    rows, bias, cells_other = lax.optimization_barrier((rows, bias, cells_other))
    early, early_other = exchange(rows)
    total = jax.ShapeDtypeStruct((ext, width), jnp.float32)
    [lifted] = local_call(
        lambda *refs: first_sum_kernel(n_x, *refs),
        (at, early, cells, early_other, cells_other, lift_weight),
        [total],
    )
    rows = pick(LATE, n_x, n_y, at, route, (u3, d3, u4, d4))
    late, late_other = exchange(rows)
    [lifted] = local_call(
        lambda *refs: next_sum_kernel(n_x, *refs), (at, lifted, late, cells, lift_weight), [total]
    )
    own_lifted, normed, sent = local_call(
        lambda *refs: last_sum_kernel(n_x, edge, *refs),
        (at, lifted, late_other, cells_other, lift_weight, norm_gain.reshape(1, -1)),
        [
            jax.ShapeDtypeStruct((own_cells, width), jnp.float32),
            jax.ShapeDtypeStruct((ext, width), jnp.bfloat16),
            jax.ShapeDtypeStruct((edge, width), jnp.bfloat16),
        ],
        [pltpu.VMEM((ext, width), jnp.float32)],
    )
    hops = [(2 * i, 2 * i - 1) for i in range(1, n_y)] + [
        (2 * i + 1, 2 * i + 2) for i in range(n_y - 1)
    ]
    far = lax.ppermute(sent, ("bevy", "cam"), hops)
    queries, keys, values = project(at, normed, w_query, w_key, w_value, own_cells)

    out = attention(
        queries, keys, values, far, w_key, w_value, bias, w_out, own_lifted
    )
    return out.reshape(ROWS_DEV, COLS_DEV, width)


def solution(mesh):
    placed = (
        P(("bevy", "bevx", "cam"), None),
        P(),
        P(("bevy", "bevx"), "cam", None, None),
        P(None, "cam", ("bevy", "bevx"), None),
        P(("bevy", "bevx"), "cam", None),
        P(),
        P(),
        P(),
        P(),
        P(),
        P(None, "bevx", None),
    )
    return jax.shard_map(
        steps,
        mesh=mesh,
        in_specs=placed,
        out_specs=P(("bevy", "cam"), "bevx", None),
        check_vma=False,
    )
```

```python
import jax
import jax.numpy as jnp
from jax import lax
from jax.experimental import pallas as pl
from jax.experimental.pallas import tpu as pltpu
from jax.sharding import PartitionSpec as P


ROWS_DEV = 8
COLS_DEV = 64
HALO = 4
MASKED = -1e30
EARLY = (0, -1, 1, -2, 2)
LATE = (-3, 3, 4)


def whole(x):
    return pl.BlockSpec(x.shape, lambda *_: (0,) * x.ndim)


SCALAR = pl.BlockSpec(memory_space=pltpu.SMEM)
LOCAL = pl.BlockSpec(memory_space=pltpu.VMEM)


def pick_kernel(offsets, n_x, at_ref, route_ref, *refs):
    blocks, out_ref = refs[:-1], refs[-1]
    used = 0
    for i, offset in enumerate(offsets):
        parts = 2 if offset == n_x // 2 else 1
        line = (at_ref[0] + (offset + n_x)) % n_x
        index = route_ref[pl.ds(line, 1), :]
        base = 0
        rows = None
        for block in blocks[used : used + parts]:
            ids = lax.broadcasted_iota(jnp.int32, (block.shape[0], index.shape[1]), 0) + base
            one_hot = jnp.where(ids == index, 1.0, 0.0).astype(jnp.bfloat16)
            got = lax.dot_general(
                one_hot,
                block[...],
                (((0,), (0,)), ((), ())),
                preferred_element_type=jnp.float32,
            )
            rows = got if rows is None else rows + got
            base += block.shape[0]
        used += parts
        out_ref[:, i] = rows.reshape(out_ref.shape[0], out_ref.shape[2], out_ref.shape[3]).astype(
            jnp.bfloat16
        )


def pick(offsets, n_x, n_y, at, route, blocks):
    slots = route.shape[1] // n_y
    width = blocks[0].shape[1]
    return pl.pallas_call(
        lambda *refs: pick_kernel(offsets, n_x, *refs),
        in_specs=[SCALAR] + [LOCAL] * (1 + len(blocks)),
        out_specs=LOCAL,
        out_shape=jax.ShapeDtypeStruct((n_y, len(offsets), slots, width), jnp.bfloat16),
        compiler_params=pltpu.CompilerParams(vmem_limit_bytes=10 << 20),
        name="pick_rows",
    )(at, route, *blocks)


def summed(offsets, n_x, at_ref, pairs, w_ref, total):
    for rows_ref, cell_ref in pairs:
        pieces = []
        hots = []
        for i, offset in enumerate(offsets):
            line = (at_ref[0] + (offset + n_x)) % n_x
            cell = cell_ref[pl.ds(line, 1), :]
            piece = rows_ref[:, i]
            pieces.append(piece.reshape(-1, piece.shape[-1]))
            ids = lax.broadcasted_iota(jnp.int32, (total.shape[0], cell.shape[1]), 0) + at_ref[1]
            hots.append(jnp.where(ids == cell, 1.0, 0.0).astype(jnp.bfloat16))
        projected = jnp.dot(
            jnp.concatenate(pieces, axis=0), w_ref[...], preferred_element_type=jnp.float32
        ).astype(jnp.bfloat16)
        total[...] += jnp.dot(
            jnp.concatenate(hots, axis=1), projected, preferred_element_type=jnp.float32
        )


def first_sum_kernel(n_x, at_ref, a_ref, ac_ref, b_ref, bc_ref, w_ref, out_ref):
    out_ref[...] = jnp.zeros_like(out_ref)
    summed(EARLY, n_x, at_ref, ((a_ref, ac_ref), (b_ref, bc_ref)), w_ref, out_ref)


def next_sum_kernel(n_x, at_ref, total_ref, a_ref, ac_ref, w_ref, out_ref):
    out_ref[...] = total_ref[...]
    summed(LATE, n_x, at_ref, ((a_ref, ac_ref),), w_ref, out_ref)


def last_sum_kernel(
    n_x, edge, at_ref, total_ref, a_ref, ac_ref, w_ref, gain_ref, own_ref, normed_ref, sent_ref, acc
):
    acc[...] = total_ref[...]
    summed(LATE, n_x, at_ref, ((a_ref, ac_ref),), w_ref, acc)
    rows = own_ref.shape[0]
    own_ref[...] = acc[pl.ds(pl.multiple_of(at_ref[1], edge), rows), :]
    for start in range(0, acc.shape[0], edge):
        lifted = acc[start : start + edge]
        mean_square = jnp.mean(lifted * lifted, axis=-1, keepdims=True)
        normed_ref[start : start + edge] = (
            lifted * lax.rsqrt(mean_square + 1e-06) * gain_ref[...]
        ).astype(jnp.bfloat16)
    sent_ref[...] = normed_ref[pl.ds(pl.multiple_of(2 * at_ref[1], edge), edge), :]


def local_call(kernel, operands, outs, scratch=()):
    return pl.pallas_call(
        kernel,
        in_specs=[SCALAR] + [LOCAL] * (len(operands) - 1),
        out_specs=[LOCAL] * len(outs),
        out_shape=outs,
        scratch_shapes=scratch,
        compiler_params=pltpu.CompilerParams(vmem_limit_bytes=16 << 20),
    )(*operands)


def project_kernel(at_ref, x_ref, wq_ref, wk_ref, wv_ref, q_ref, k_ref, v_ref):
    rows = q_ref.shape[0]
    own = x_ref[pl.ds(pl.multiple_of(at_ref[1], rows // 2), rows), :]
    x = x_ref[...]
    q_ref[...] = (jnp.dot(own, wq_ref[...], preferred_element_type=jnp.float32)).astype(
        jnp.bfloat16
    )
    k_ref[...] = jnp.dot(x, wk_ref[...], preferred_element_type=jnp.float32).astype(jnp.bfloat16)
    v_ref[...] = jnp.dot(x, wv_ref[...], preferred_element_type=jnp.float32).astype(jnp.bfloat16)


def project(at, x, w_query, w_key, w_value, rows):
    ext, width = x.shape
    block = 256
    column = lambda r: pl.BlockSpec((r, block), lambda i: (0, i))
    return pl.pallas_call(
        project_kernel,
        grid=(width // block,),
        in_specs=[SCALAR, whole(x)] + [column(width)] * 3,
        out_specs=[column(rows), column(ext), column(ext)],
        out_shape=[
            jax.ShapeDtypeStruct((r, width), jnp.bfloat16) for r in (rows, ext, ext)
        ],
        compiler_params=pltpu.CompilerParams(
            dimension_semantics=("arbitrary",), vmem_limit_bytes=16 << 20
        ),
        name="near_projections",
    )(at, x, w_query, w_key, w_value)


def attention_kernel(
    q_ref, k_ref, v_ref, far_ref, wk_ref, wv_ref, bias_ref, wo_ref, lifted_ref, out_ref, att_ref
):
    step = pl.program_id(0)
    rows_q = q_ref.shape[0]
    chunk = rows_q
    far = far_ref[...]
    far_k = jnp.dot(far, wk_ref[...], preferred_element_type=jnp.float32).astype(jnp.bfloat16)
    far_v = jnp.dot(far, wv_ref[...], preferred_element_type=jnp.float32).astype(jnp.bfloat16)
    lane = lax.broadcasted_iota(jnp.int32, (chunk, 128), 1)
    for pair in range(2):
        cut = slice(pair * 128, pair * 128 + 128)
        k = jnp.concatenate([k_ref[:, cut], far_k[:, cut]], axis=0)
        v = jnp.concatenate([v_ref[:, cut], far_v[:, cut]], axis=0)
        keys = jnp.concatenate([k, bias_ref[...]], axis=1)
        values = jnp.concatenate([v, jnp.ones_like(v)], axis=1)
        for start in range(0, rows_q, chunk):
            q = q_ref[start : start + chunk, cut] * jnp.asarray(0.125, jnp.bfloat16)
            done = []
            for side in range(2):
                own = (lane >= 64) if side else (lane < 64)
                query = jnp.concatenate(
                    [
                        jnp.where(own, q, jnp.zeros((), jnp.bfloat16)),
                        jnp.where(lane == 4 * step + 2 * pair + side, 1.0, 0.0).astype(
                            jnp.bfloat16
                        ),
                    ],
                    axis=1,
                )
                score = lax.dot_general(
                    query, keys, (((1,), (1,)), ((), ())), preferred_element_type=jnp.float32
                )
                top = jnp.max(score, axis=1, keepdims=True)
                weight = jnp.exp(score - top).astype(jnp.bfloat16)
                total = jnp.dot(weight, values, preferred_element_type=jnp.float32)
                done.append(total[:, :128] / total[:, 128:])
            att_ref[2 * step + pair, start : start + chunk] = jnp.where(
                lane < 64, done[0], done[1]
            ).astype(jnp.bfloat16)

    @pl.when(step == pl.num_programs(0) - 1)
    def _():
        attended = jnp.concatenate([att_ref[i] for i in range(att_ref.shape[0])], axis=1)
        mixed = jnp.dot(attended, wo_ref[...], preferred_element_type=jnp.float32)
        out_ref[...] = (lifted_ref[...] + mixed).astype(jnp.bfloat16)


def attention(q, k, v, far, w_key, w_value, bias, w_out, lifted):
    rows, width = q.shape
    block = 256
    column = lambda x: pl.BlockSpec((x.shape[0], block), lambda i: (0, i))
    return pl.pallas_call(
        attention_kernel,
        grid=(width // block,),
        in_specs=[
            column(q),
            column(k),
            column(v),
            whole(far),
            column(w_key),
            column(w_value),
            whole(bias),
            whole(w_out),
            whole(lifted),
        ],
        out_specs=pl.BlockSpec((rows, width), lambda i: (0, 0)),
        out_shape=jax.ShapeDtypeStruct((rows, width), jnp.bfloat16),
        scratch_shapes=[pltpu.VMEM((width // 128, rows, 128), jnp.bfloat16)],
        compiler_params=pltpu.CompilerParams(
            dimension_semantics=("arbitrary",), vmem_limit_bytes=40 << 20
        ),
        name="window_attention",
    )(q, k, v, far, w_key, w_value, bias, w_out, lifted)


def steps(
    image_tokens,
    lift_weight,
    route_token,
    route_cell,
    slot_counts,
    norm_gain,
    w_query,
    w_key,
    w_value,
    w_out,
    key_bias,
):
    n_y = lax.axis_size("bevy")
    n_x = lax.axis_size("bevx")
    slot_count = route_token.shape[3]
    tokens = image_tokens.shape[0]
    width = lift_weight.shape[1]
    head_count = key_bias.shape[2]
    grid_rows = key_bias.shape[0]
    own_cells = ROWS_DEV * COLS_DEV
    edge = HALO * COLS_DEV
    ext = own_cells + edge
    row = lax.axis_index("bevy")
    col = lax.axis_index("bevx")
    core = lax.axis_index("cam")
    up = [(i, (i + 1) % n_x) for i in range(n_x)]
    down = [(b, a) for a, b in up]
    swap = [(0, 1), (1, 0)]
    at = jnp.stack([col, core * edge]).astype(jnp.int32)

    def shift(value, perm):
        return lax.ppermute(value, "bevx", perm)

    u1 = shift(image_tokens, up)
    d1 = shift(image_tokens, down)

    def by_column(value):
        return value.reshape(n_y, n_x, slot_count).transpose(1, 0, 2).reshape(n_x, -1)

    is_live = (
        lax.broadcasted_iota(jnp.int32, route_token.shape[2:], 1) < slot_counts[0, 0][:, None]
    )
    route = by_column(jnp.where(is_live, route_token[0, 0], -1))
    cells = by_column(route_cell[:, 0, 0, :])
    route, cells = lax.optimization_barrier((route, cells))
    cells_other = lax.ppermute(cells, "cam", swap)
    route = lax.all_to_all(route, "bevx", split_axis=0, concat_axis=0, tiled=True)

    u2 = shift(u1, up)
    d2 = shift(d1, down)
    u3 = shift(u2, up)
    d3 = shift(d2, down)
    half = tokens // 2
    u4 = shift(u3[:half], up)
    d4 = shift(d3[half:], down)

    near_row = (row * 2 + core) * ROWS_DEV - core * HALO
    far_row = (row * 2 + core) * ROWS_DEV + jnp.where(core == 0, -HALO, ROWS_DEV)
    far_ok = (far_row >= 0) & (far_row < grid_rows)
    near_bias = lax.dynamic_slice_in_dim(key_bias, near_row, ROWS_DEV + HALO, 0)
    far_bias = lax.dynamic_slice_in_dim(
        key_bias, jnp.clip(far_row, 0, grid_rows - HALO), HALO, 0
    )
    far_bias = jnp.where(far_ok, far_bias, jnp.asarray(MASKED, jnp.bfloat16))
    bias = jnp.concatenate([near_bias, far_bias], axis=0).reshape(-1, head_count)
    bias = jnp.pad(bias, ((0, 0), (0, 128 - head_count)))

    def exchange(rows):
        got = lax.all_to_all(rows, "bevy", split_axis=0, concat_axis=0, tiled=True)
        return got, lax.ppermute(got, "cam", swap)

    rows = pick(EARLY, n_x, n_y, at, route, (image_tokens, u1, d1, u2, d2))
    rows, bias, cells_other = lax.optimization_barrier((rows, bias, cells_other))
    early, early_other = exchange(rows)
    total = jax.ShapeDtypeStruct((ext, width), jnp.float32)
    [lifted] = local_call(
        lambda *refs: first_sum_kernel(n_x, *refs),
        (at, early, cells, early_other, cells_other, lift_weight),
        [total],
    )
    rows = pick(LATE, n_x, n_y, at, route, (u3, d3, u4, d4))
    late, late_other = exchange(rows)
    [lifted] = local_call(
        lambda *refs: next_sum_kernel(n_x, *refs), (at, lifted, late, cells, lift_weight), [total]
    )
    own_lifted, normed, sent = local_call(
        lambda *refs: last_sum_kernel(n_x, edge, *refs),
        (at, lifted, late_other, cells_other, lift_weight, norm_gain.reshape(1, -1)),
        [
            jax.ShapeDtypeStruct((own_cells, width), jnp.float32),
            jax.ShapeDtypeStruct((ext, width), jnp.bfloat16),
            jax.ShapeDtypeStruct((edge, width), jnp.bfloat16),
        ],
        [pltpu.VMEM((ext, width), jnp.float32)],
    )
    hops = [(2 * i, 2 * i - 1) for i in range(1, n_y)] + [
        (2 * i + 1, 2 * i + 2) for i in range(n_y - 1)
    ]
    far = lax.ppermute(sent, ("bevy", "cam"), hops)
    queries, keys, values = project(at, normed, w_query, w_key, w_value, own_cells)

    out = attention(
        queries, keys, values, far, w_key, w_value, bias, w_out, own_lifted
    )
    return out.reshape(ROWS_DEV, COLS_DEV, width)


def solution(mesh):
    placed = (
        P(("bevy", "bevx", "cam"), None),
        P(),
        P(("bevy", "bevx"), "cam", None, None),
        P(None, "cam", ("bevy", "bevx"), None),
        P(("bevy", "bevx"), "cam", None),
        P(),
        P(),
        P(),
        P(),
        P(),
        P(None, "bevx", None),
    )
    return jax.shard_map(
        steps,
        mesh=mesh,
        in_specs=placed,
        out_specs=P(("bevy", "cam"), "bevx", None),
        check_vma=False,
    )
```

```python
import jax
import jax.numpy as jnp
from jax import lax
from jax.experimental import pallas as pl
from jax.experimental.pallas import tpu as pltpu
from jax.sharding import PartitionSpec as P


ROWS_DEV = 8
COLS_DEV = 64
HALO = 4
MASKED = -1e30
HEAD_LANES = 16
EARLY = (0, -1, 1, -2, 2)
LATE = (-3, 3, 4)


SCALAR = pl.BlockSpec(memory_space=pltpu.SMEM)
LOCAL = pl.BlockSpec(memory_space=pltpu.VMEM)


def pick_kernel(offsets, n_x, at_ref, route_ref, *refs):
    blocks, out_ref = refs[:-1], refs[-1]
    used = 0
    for i, offset in enumerate(offsets):
        parts = 2 if offset == n_x // 2 else 1
        line = (at_ref[0] + (offset + n_x)) % n_x
        index = route_ref[pl.ds(line, 1), :]
        base = 0
        rows = None
        for block in blocks[used : used + parts]:
            ids = lax.broadcasted_iota(jnp.int32, (block.shape[0], index.shape[1]), 0) + base
            one_hot = jnp.where(ids == index, 1.0, 0.0).astype(jnp.bfloat16)
            got = lax.dot_general(
                one_hot,
                block[...],
                (((0,), (0,)), ((), ())),
                preferred_element_type=jnp.float32,
            )
            rows = got if rows is None else rows + got
            base += block.shape[0]
        used += parts
        out_ref[:, i] = rows.reshape(out_ref.shape[0], out_ref.shape[2], out_ref.shape[3]).astype(
            jnp.bfloat16
        )


def pick(offsets, n_x, n_y, at, route, blocks):
    slots = route.shape[1] // n_y
    width = blocks[0].shape[1]
    return pl.pallas_call(
        lambda *refs: pick_kernel(offsets, n_x, *refs),
        in_specs=[SCALAR] + [LOCAL] * (1 + len(blocks)),
        out_specs=LOCAL,
        out_shape=jax.ShapeDtypeStruct((n_y, len(offsets), slots, width), jnp.bfloat16),
        compiler_params=pltpu.CompilerParams(vmem_limit_bytes=10 << 20),
        name="pick_rows",
    )(at, route, *blocks)


def summed(offsets, n_x, at_ref, pairs, w_ref, total, ready=None):
    for rows_ref, cell_ref in pairs:
        pieces = []
        hots = []
        for i, offset in enumerate(offsets):
            line = (at_ref[0] + (offset + n_x)) % n_x
            cell = cell_ref[pl.ds(line, 1), :]
            piece = rows_ref[:, i]
            pieces.append(piece.reshape(-1, piece.shape[-1]))
            ids = lax.broadcasted_iota(jnp.int32, (total.shape[0], cell.shape[1]), 0) + at_ref[1]
            hots.append(jnp.where(ids == cell, 1.0, 0.0).astype(jnp.bfloat16))
        projected = jnp.dot(
            jnp.concatenate(pieces, axis=0), w_ref[...], preferred_element_type=jnp.float32
        ).astype(jnp.bfloat16)
        added = jnp.dot(
            jnp.concatenate(hots, axis=1), projected, preferred_element_type=jnp.float32
        )
        if ready is not None:
            ready()
        total[...] += added


def first_sum_kernel(n_x, at_ref, a_ref, ac_ref, w_ref, out_ref):
    out_ref[...] = jnp.zeros_like(out_ref)
    summed(EARLY, n_x, at_ref, ((a_ref, ac_ref),), w_ref, out_ref)


def second_sum_kernel(n_x, at_ref, total_ref, a_ref, ac_ref, w_ref, out_ref):
    out_ref[...] = total_ref[...]
    summed(EARLY, n_x, at_ref, ((a_ref, ac_ref),), w_ref, out_ref)


def next_sum_kernel(n_x, at_ref, total_ref, a_ref, ac_ref, w_ref, out_ref, sem):
    copy = pltpu.make_async_copy(total_ref, out_ref, sem)
    copy.start()
    summed(LATE, n_x, at_ref, ((a_ref, ac_ref),), w_ref, out_ref, copy.wait)


def last_sum_kernel(
    n_x, edge, at_ref, total_ref, a_ref, ac_ref, w_ref, gain_ref, own_ref, normed_ref, sent_ref, acc
):
    acc[...] = total_ref[...]
    summed(LATE, n_x, at_ref, ((a_ref, ac_ref),), w_ref, acc)
    rows = own_ref.shape[0]
    own_ref[...] = acc[pl.ds(pl.multiple_of(at_ref[1], edge), rows), :]
    for start in range(0, acc.shape[0], edge):
        lifted = acc[start : start + edge]
        mean_square = jnp.mean(lifted * lifted, axis=-1, keepdims=True)
        normed_ref[start : start + edge] = (
            lifted * lax.rsqrt(mean_square + 1e-06) * gain_ref[...]
        ).astype(jnp.bfloat16)
    sent_ref[...] = normed_ref[pl.ds(pl.multiple_of(2 * at_ref[1], edge), edge), :]


def local_call(kernel, operands, outs, scratch=(), remote=()):
    return pl.pallas_call(
        kernel,
        in_specs=[SCALAR]
        + [
            pl.BlockSpec(memory_space=pltpu.HBM) if i in remote else LOCAL
            for i in range(1, len(operands))
        ],
        out_specs=[LOCAL] * len(outs),
        out_shape=outs,
        scratch_shapes=scratch,
        compiler_params=pltpu.CompilerParams(vmem_limit_bytes=16 << 20),
    )(*operands)


def flipped(w, x):
    return jnp.dot(x, w, preferred_element_type=jnp.float32).T


def project_kernel(at_ref, x_ref, wq_ref, wk_ref, wv_ref, q_ref, k_ref, v_ref):
    rows = q_ref.shape[0]
    own = x_ref[pl.ds(pl.multiple_of(at_ref[1], rows // 2), rows), :]
    x = x_ref[...]
    q_ref[...] = (jnp.dot(own, wq_ref[...], preferred_element_type=jnp.float32)).astype(
        jnp.bfloat16
    )
    k_ref[...] = jnp.dot(x, wk_ref[...], preferred_element_type=jnp.float32).astype(jnp.bfloat16)
    v_ref[...] = flipped(wv_ref[...], x).astype(jnp.bfloat16)


def project(at, x, w_query, w_key, w_value, rows):
    ext, width = x.shape
    return pl.pallas_call(
        project_kernel,
        in_specs=[SCALAR] + [LOCAL] * 4,
        out_specs=[LOCAL] * 3,
        out_shape=[
            jax.ShapeDtypeStruct(shape, jnp.bfloat16)
            for shape in ((rows, width), (ext, width), (width, ext))
        ],
        compiler_params=pltpu.CompilerParams(vmem_limit_bytes=24 << 20),
        name="near_projections",
    )(at, x, w_query, w_key, w_value)


def attention_kernel(
    q_ref, k_ref, v_ref, far_ref, wk_ref, wv_ref, bias_ref, wo_ref, lifted_ref, out_ref, att_ref,
    far_k_ref, far_v_ref,
):
    step = pl.program_id(0)
    rows_q = q_ref.shape[0]
    size = 64
    heads = att_ref.shape[1] // size
    here = pl.ds(pl.multiple_of(step * att_ref.shape[1], 256), att_ref.shape[1])
    q_ref = q_ref.at[:, here]
    k_ref = k_ref.at[:, here]
    v_ref = v_ref.at[here, :]
    wk_ref = wk_ref.at[:, here]
    wv_ref = wv_ref.at[:, here]
    far = far_ref[...]
    far_k_ref[...] = jnp.dot(far, wk_ref[...], preferred_element_type=jnp.float32).astype(
        jnp.bfloat16
    )
    far_v_ref[...] = flipped(wv_ref[...], far).astype(jnp.bfloat16)
    lane = lax.broadcasted_iota(jnp.int32, (rows_q, 128), 1)
    tops = jnp.max(bias_ref[...].astype(jnp.float32), axis=0, keepdims=True)
    lane_top = lax.broadcasted_iota(jnp.int32, tops.shape, 1)

    def scored(head, pair, side):
        cut = pl.ds(pair * 128, 128)
        k = jnp.concatenate([k_ref[:, cut], far_k_ref[:, cut]], axis=0)
        keys = jnp.concatenate([k, bias_ref[...]], axis=1)
        q = q_ref[:, cut] * jnp.asarray(0.125, jnp.bfloat16)
        mine = (lane // size) == side
        number = heads * step + head
        top = jnp.max(jnp.where(lane_top == number, tops, -jnp.inf), axis=1, keepdims=True)
        extra = jnp.where(lane == number, 1.0, jnp.where(lane == HEAD_LANES, -top, 0.0))
        query = jnp.concatenate(
            [jnp.where(mine, q, jnp.zeros((), jnp.bfloat16)), extra.astype(jnp.bfloat16)],
            axis=1,
        )
        return lax.dot_general(
            keys, query, (((1,), (1,)), ((), ())), preferred_element_type=jnp.float32
        )

    def weighed(own, weight):
        v = jnp.concatenate([v_ref[own, :], far_v_ref[own, :]], axis=1)
        values = jnp.concatenate([v, jnp.ones((16, v.shape[1]), jnp.bfloat16)], axis=0)
        mixed = jnp.dot(values, weight, preferred_element_type=jnp.float32)
        total = mixed[size : size + 1]
        att_ref[step, own, :] = (mixed[:size] / total).astype(jnp.bfloat16)
        return total

    least = most = None
    scores = [scored(0, 0, 0)]
    for head in range(heads):
        if head + 1 < heads:
            scores.append(scored(head + 1, (head + 1) // 2, (head + 1) % 2))
        total = weighed(
            slice(head * size, head * size + size), jnp.exp(scores[head]).astype(jnp.bfloat16)
        )
        least = total if head == 0 else jnp.minimum(least, total)
        most = total if head == 0 else jnp.maximum(most, total)
    safe = (jnp.min(least) > 1e-18) & (jnp.max(most) < 1e30)

    @pl.when(jnp.logical_not(safe))
    def _():
        def again(head, carry):
            score = scored(head, head // 2, head % 2)
            weight = jnp.exp(score - jnp.max(score, axis=0, keepdims=True)).astype(jnp.bfloat16)
            weighed(pl.ds(pl.multiple_of(head * size, size), size), weight)
            return carry

        lax.fori_loop(0, heads, again, 0)

    @pl.when(step == pl.num_programs(0) - 1)
    def _():
        attended = att_ref[...].reshape(-1, rows_q)
        mixed = lax.dot_general(
            attended, wo_ref[...], (((0,), (0,)), ((), ())), preferred_element_type=jnp.float32
        )
        out_ref[...] = (lifted_ref[...] + mixed).astype(jnp.bfloat16)


def attention(q, k, v, far, w_key, w_value, bias, w_out, lifted):
    rows, width = q.shape
    block = 256
    return pl.pallas_call(
        attention_kernel,
        grid=(width // block,),
        in_specs=[LOCAL] * 9,
        out_specs=LOCAL,
        out_shape=jax.ShapeDtypeStruct((rows, width), jnp.bfloat16),
        scratch_shapes=[
            pltpu.VMEM((width // block, block, rows), jnp.bfloat16),
            pltpu.VMEM((far.shape[0], block), jnp.bfloat16),
            pltpu.VMEM((block, far.shape[0]), jnp.bfloat16),
        ],
        compiler_params=pltpu.CompilerParams(
            dimension_semantics=("arbitrary",), vmem_limit_bytes=28 << 20
        ),
        name="window_attention",
    )(q, k, v, far, w_key, w_value, bias, w_out, lifted)


def steps(
    image_tokens,
    lift_weight,
    route_token,
    route_cell,
    slot_counts,
    norm_gain,
    w_query,
    w_key,
    w_value,
    w_out,
    key_bias,
):
    n_y = lax.axis_size("bevy")
    n_x = lax.axis_size("bevx")
    slot_count = route_token.shape[3]
    tokens = image_tokens.shape[0]
    width = lift_weight.shape[1]
    head_count = key_bias.shape[2]
    grid_rows = key_bias.shape[0]
    own_cells = ROWS_DEV * COLS_DEV
    edge = HALO * COLS_DEV
    ext = own_cells + edge
    row = lax.axis_index("bevy")
    col = lax.axis_index("bevx")
    core = lax.axis_index("cam")
    up = [(i, (i + 1) % n_x) for i in range(n_x)]
    down = [(b, a) for a, b in up]
    swap = [(0, 1), (1, 0)]
    at = jnp.stack([col, core * edge]).astype(jnp.int32)

    def shift(value, perm):
        return lax.ppermute(value, "bevx", perm)

    u1 = shift(image_tokens, up)
    d1 = shift(image_tokens, down)

    def by_column(value):
        return value.reshape(n_y, n_x, slot_count).transpose(1, 0, 2).reshape(n_x, -1)

    is_live = (
        lax.broadcasted_iota(jnp.int32, route_token.shape[2:], 1) < slot_counts[0, 0][:, None]
    )
    route = by_column(jnp.where(is_live, route_token[0, 0], -1))
    cells = by_column(route_cell[:, 0, 0, :])
    route, cells = lax.optimization_barrier((route, cells))
    cells_other = lax.ppermute(cells, "cam", swap)
    route = lax.all_to_all(route, "bevx", split_axis=0, concat_axis=0, tiled=True)

    u2 = shift(u1, up)
    d2 = shift(d1, down)
    u3 = shift(u2, up)
    d3 = shift(d2, down)
    half = tokens // 2
    u4 = shift(u3[:half], up)
    d4 = shift(d3[half:], down)

    near_row = (row * 2 + core) * ROWS_DEV - core * HALO
    far_row = (row * 2 + core) * ROWS_DEV + jnp.where(core == 0, -HALO, ROWS_DEV)
    far_ok = (far_row >= 0) & (far_row < grid_rows)
    near_bias = lax.dynamic_slice_in_dim(key_bias, near_row, ROWS_DEV + HALO, 0)
    far_bias = lax.dynamic_slice_in_dim(
        key_bias, jnp.clip(far_row, 0, grid_rows - HALO), HALO, 0
    )
    far_bias = jnp.where(far_ok, far_bias, jnp.asarray(MASKED, jnp.bfloat16))
    bias = jnp.concatenate([near_bias, far_bias], axis=0).reshape(-1, head_count)
    bias = jnp.pad(bias, ((0, 0), (0, 1)), constant_values=1)
    bias = jnp.pad(bias, ((0, 0), (0, 127 - head_count)))

    def exchange(rows):
        got = lax.all_to_all(rows, "bevy", split_axis=0, concat_axis=0, tiled=True)
        return got, lax.ppermute(got, "cam", swap)

    rows = pick(EARLY, n_x, n_y, at, route, (image_tokens, u1, d1, u2, d2))
    rows, bias, cells_other = lax.optimization_barrier((rows, bias, cells_other))
    early, early_other = exchange(rows)
    total = jax.ShapeDtypeStruct((ext, width), jnp.float32)
    [lifted] = local_call(
        lambda *refs: first_sum_kernel(n_x, *refs), (at, early, cells, lift_weight), [total]
    )
    [lifted] = local_call(
        lambda *refs: second_sum_kernel(n_x, *refs),
        (at, lifted, early_other, cells_other, lift_weight),
        [total],
    )
    rows = pick(LATE, n_x, n_y, at, route, (u3, d3, u4, d4))
    late, late_other = exchange(rows)
    [lifted] = local_call(
        lambda *refs: next_sum_kernel(n_x, *refs),
        (
            at,
            pltpu.with_memory_space_constraint(lifted, pltpu.HBM),
            late,
            cells,
            lift_weight,
        ),
        [total],
        [pltpu.SemaphoreType.DMA],
        (1,),
    )
    own_lifted, normed, sent = local_call(
        lambda *refs: last_sum_kernel(n_x, edge, *refs),
        (at, lifted, late_other, cells_other, lift_weight, norm_gain.reshape(1, -1)),
        [
            jax.ShapeDtypeStruct((own_cells, width), jnp.float32),
            jax.ShapeDtypeStruct((ext, width), jnp.bfloat16),
            jax.ShapeDtypeStruct((edge, width), jnp.bfloat16),
        ],
        [pltpu.VMEM((ext, width), jnp.float32)],
    )
    hops = [(2 * i, 2 * i - 1) for i in range(1, n_y)] + [
        (2 * i + 1, 2 * i + 2) for i in range(n_y - 1)
    ]
    far = lax.ppermute(sent, ("bevy", "cam"), hops)
    queries, keys, values = project(at, normed, w_query, w_key, w_value, own_cells)

    out = attention(
        queries, keys, values, far, w_key, w_value, bias, w_out, own_lifted
    )
    return out.reshape(ROWS_DEV, COLS_DEV, width)


def solution(mesh):
    placed = (
        P(("bevy", "bevx", "cam"), None),
        P(),
        P(("bevy", "bevx"), "cam", None, None),
        P(None, "cam", ("bevy", "bevx"), None),
        P(("bevy", "bevx"), "cam", None),
        P(),
        P(),
        P(),
        P(),
        P(),
        P(None, "bevx", None),
    )
    return jax.shard_map(
        steps,
        mesh=mesh,
        in_specs=placed,
        out_specs=P(("bevy", "cam"), "bevx", None),
        check_vma=False,
    )
```

```python
import jax
import jax.numpy as jnp
from jax import lax
from jax.experimental import pallas as pl
from jax.experimental.pallas import tpu as pltpu
from jax.sharding import PartitionSpec as P


ROWS_DEV = 8
COLS_DEV = 64
HALO = 4
MASKED = -1e30
HEAD_LANES = 16
ONE = (0, -1, 1)
TWO = (-2, 2)
LATE = (-3, 3, 4)


SCALAR = pl.BlockSpec(memory_space=pltpu.SMEM)
LOCAL = pl.BlockSpec(memory_space=pltpu.VMEM)


def pick_kernel(offsets, n_x, at_ref, route_ref, *refs):
    blocks, out_ref = refs[:-1], refs[-1]
    used = 0
    for i, offset in enumerate(offsets):
        parts = 2 if offset == n_x // 2 else 1
        line = (at_ref[0] + (offset + n_x)) % n_x
        index = route_ref[pl.ds(line, 1), :]
        base = 0
        rows = None
        for block in blocks[used : used + parts]:
            ids = lax.broadcasted_iota(jnp.int32, (block.shape[0], index.shape[1]), 0) + base
            one_hot = jnp.where(ids == index, 1.0, 0.0).astype(jnp.bfloat16)
            got = lax.dot_general(
                one_hot,
                block[...],
                (((0,), (0,)), ((), ())),
                preferred_element_type=jnp.float32,
            )
            rows = got if rows is None else rows + got
            base += block.shape[0]
        used += parts
        out_ref[:, i] = rows.reshape(out_ref.shape[0], out_ref.shape[2], out_ref.shape[3]).astype(
            jnp.bfloat16
        )


def pick(offsets, n_x, n_y, at, route, blocks):
    slots = route.shape[1] // n_y
    width = blocks[0].shape[1]
    return pl.pallas_call(
        lambda *refs: pick_kernel(offsets, n_x, *refs),
        in_specs=[SCALAR] + [LOCAL] * (1 + len(blocks)),
        out_specs=LOCAL,
        out_shape=jax.ShapeDtypeStruct((n_y, len(offsets), slots, width), jnp.bfloat16),
        compiler_params=pltpu.CompilerParams(vmem_limit_bytes=10 << 20),
        name="pick_rows",
    )(at, route, *blocks)


def summed(offsets, n_x, at_ref, pairs, w_ref, total, ready=None):
    for rows_ref, cell_ref in pairs:
        pieces = []
        hots = []
        for i, offset in enumerate(offsets):
            line = (at_ref[0] + (offset + n_x)) % n_x
            cell = cell_ref[pl.ds(line, 1), :]
            piece = rows_ref[:, i]
            pieces.append(piece.reshape(-1, piece.shape[-1]))
            ids = lax.broadcasted_iota(jnp.int32, (total.shape[0], cell.shape[1]), 0) + at_ref[1]
            hots.append(jnp.where(ids == cell, 1.0, 0.0).astype(jnp.bfloat16))
        projected = jnp.dot(
            jnp.concatenate(pieces, axis=0), w_ref[...], preferred_element_type=jnp.float32
        ).astype(jnp.bfloat16)
        added = jnp.dot(
            jnp.concatenate(hots, axis=1), projected, preferred_element_type=jnp.float32
        )
        if ready is not None:
            ready()
        total[...] += added


def start_sum_kernel(n_x, at_ref, a_ref, ac_ref, b_ref, bc_ref, w_ref, out_ref):
    out_ref[...] = jnp.zeros_like(out_ref)
    summed(ONE, n_x, at_ref, ((a_ref, ac_ref), (b_ref, bc_ref)), w_ref, out_ref)


def next_sum_kernel(offsets, n_x, at_ref, total_ref, *refs):
    pairs, (w_ref, out_ref, sem) = refs[:-3], refs[-3:]
    copy = pltpu.make_async_copy(total_ref, out_ref, sem)
    copy.start()
    for i in range(0, len(pairs), 2):
        ready = copy.wait if i == 0 else None
        summed(offsets, n_x, at_ref, (pairs[i : i + 2],), w_ref, out_ref, ready)


def last_sum_kernel(
    n_x, edge, at_ref, total_ref, a_ref, ac_ref, w_ref, gain_ref, own_ref, normed_ref, sent_ref, acc
):
    acc[...] = total_ref[...]
    summed(LATE, n_x, at_ref, ((a_ref, ac_ref),), w_ref, acc)
    rows = own_ref.shape[0]
    own_ref[...] = acc[pl.ds(pl.multiple_of(at_ref[1], edge), rows), :]
    for start in range(0, acc.shape[0], edge):
        lifted = acc[start : start + edge]
        mean_square = jnp.mean(lifted * lifted, axis=-1, keepdims=True)
        normed_ref[start : start + edge] = (
            lifted * lax.rsqrt(mean_square + 1e-06) * gain_ref[...]
        ).astype(jnp.bfloat16)
    sent_ref[...] = normed_ref[pl.ds(pl.multiple_of(2 * at_ref[1], edge), edge), :]


def local_call(kernel, operands, outs, scratch=(), remote=()):
    return pl.pallas_call(
        kernel,
        in_specs=[SCALAR]
        + [
            pl.BlockSpec(memory_space=pltpu.HBM) if i in remote else LOCAL
            for i in range(1, len(operands))
        ],
        out_specs=[LOCAL] * len(outs),
        out_shape=outs,
        scratch_shapes=scratch,
        compiler_params=pltpu.CompilerParams(vmem_limit_bytes=16 << 20),
    )(*operands)


def flipped(w, x):
    return jnp.dot(x, w, preferred_element_type=jnp.float32).T


def project_kernel(at_ref, x_ref, wq_ref, wk_ref, wv_ref, q_ref, k_ref, v_ref):
    rows = q_ref.shape[0]
    own = x_ref[pl.ds(pl.multiple_of(at_ref[1], rows // 2), rows), :]
    x = x_ref[...]
    q_ref[...] = (jnp.dot(own, wq_ref[...], preferred_element_type=jnp.float32)).astype(
        jnp.bfloat16
    )
    k_ref[...] = jnp.dot(x, wk_ref[...], preferred_element_type=jnp.float32).astype(jnp.bfloat16)
    v_ref[...] = flipped(wv_ref[...], x).astype(jnp.bfloat16)


def project(at, x, w_query, w_key, w_value, rows):
    ext, width = x.shape
    return pl.pallas_call(
        project_kernel,
        in_specs=[SCALAR] + [LOCAL] * 4,
        out_specs=[LOCAL] * 3,
        out_shape=[
            jax.ShapeDtypeStruct(shape, jnp.bfloat16)
            for shape in ((rows, width), (ext, width), (width, ext))
        ],
        compiler_params=pltpu.CompilerParams(vmem_limit_bytes=24 << 20),
        name="near_projections",
    )(at, x, w_query, w_key, w_value)


def attention_kernel(
    q_ref, k_ref, v_ref, far_ref, wk_ref, wv_ref, bias_ref, wo_ref, lifted_ref, out_ref, att_ref,
    far_k_ref, far_v_ref,
):
    step = pl.program_id(0)
    rows_q = q_ref.shape[0]
    size = 64
    heads = att_ref.shape[1] // size
    here = pl.ds(pl.multiple_of(step * att_ref.shape[1], 256), att_ref.shape[1])
    q_ref = q_ref.at[:, here]
    k_ref = k_ref.at[:, here]
    v_ref = v_ref.at[here, :]
    wk_ref = wk_ref.at[:, here]
    wv_ref = wv_ref.at[:, here]
    far = far_ref[...]
    far_k_ref[...] = jnp.dot(far, wk_ref[...], preferred_element_type=jnp.float32).astype(
        jnp.bfloat16
    )
    far_v_ref[...] = flipped(wv_ref[...], far).astype(jnp.bfloat16)
    lane = lax.broadcasted_iota(jnp.int32, (rows_q, 128), 1)
    tops = jnp.max(bias_ref[...].astype(jnp.float32), axis=0, keepdims=True)
    lane_top = lax.broadcasted_iota(jnp.int32, tops.shape, 1)

    def scored(head, pair, side):
        cut = pl.ds(pair * 128, 128)
        k = jnp.concatenate([k_ref[:, cut], far_k_ref[:, cut]], axis=0)
        keys = jnp.concatenate([k, bias_ref[...]], axis=1)
        q = q_ref[:, cut] * jnp.asarray(0.125, jnp.bfloat16)
        mine = (lane // size) == side
        number = heads * step + head
        top = jnp.max(jnp.where(lane_top == number, tops, -jnp.inf), axis=1, keepdims=True)
        extra = jnp.where(lane == number, 1.0, jnp.where(lane == HEAD_LANES, -top, 0.0))
        query = jnp.concatenate(
            [jnp.where(mine, q, jnp.zeros((), jnp.bfloat16)), extra.astype(jnp.bfloat16)],
            axis=1,
        )
        return lax.dot_general(
            keys, query, (((1,), (1,)), ((), ())), preferred_element_type=jnp.float32
        )

    def weighed(own, weight):
        v = jnp.concatenate([v_ref[own, :], far_v_ref[own, :]], axis=1)
        values = jnp.concatenate([v, jnp.ones((16, v.shape[1]), jnp.bfloat16)], axis=0)
        mixed = jnp.dot(values, weight, preferred_element_type=jnp.float32)
        total = mixed[size : size + 1]
        att_ref[step, own, :] = (mixed[:size] / total).astype(jnp.bfloat16)
        return total

    least = most = None
    scores = [scored(0, 0, 0)]
    for head in range(heads):
        if head + 1 < heads:
            scores.append(scored(head + 1, (head + 1) // 2, (head + 1) % 2))
        total = weighed(
            slice(head * size, head * size + size), jnp.exp(scores[head]).astype(jnp.bfloat16)
        )
        least = total if head == 0 else jnp.minimum(least, total)
        most = total if head == 0 else jnp.maximum(most, total)
    safe = (jnp.min(least) > 1e-18) & (jnp.max(most) < 1e30)

    @pl.when(jnp.logical_not(safe))
    def _():
        def again(head, carry):
            score = scored(head, head // 2, head % 2)
            weight = jnp.exp(score - jnp.max(score, axis=0, keepdims=True)).astype(jnp.bfloat16)
            weighed(pl.ds(pl.multiple_of(head * size, size), size), weight)
            return carry

        lax.fori_loop(0, heads, again, 0)

    @pl.when(step == pl.num_programs(0) - 1)
    def _():
        attended = att_ref[...].reshape(-1, rows_q)
        mixed = lax.dot_general(
            attended, wo_ref[...], (((0,), (0,)), ((), ())), preferred_element_type=jnp.float32
        )
        out_ref[...] = (lifted_ref[...] + mixed).astype(jnp.bfloat16)


def attention(q, k, v, far, w_key, w_value, bias, w_out, lifted):
    rows, width = q.shape
    block = 256
    return pl.pallas_call(
        attention_kernel,
        grid=(width // block,),
        in_specs=[LOCAL] * 9,
        out_specs=LOCAL,
        out_shape=jax.ShapeDtypeStruct((rows, width), jnp.bfloat16),
        scratch_shapes=[
            pltpu.VMEM((width // block, block, rows), jnp.bfloat16),
            pltpu.VMEM((far.shape[0], block), jnp.bfloat16),
            pltpu.VMEM((block, far.shape[0]), jnp.bfloat16),
        ],
        compiler_params=pltpu.CompilerParams(
            dimension_semantics=("arbitrary",), vmem_limit_bytes=28 << 20
        ),
        name="window_attention",
    )(q, k, v, far, w_key, w_value, bias, w_out, lifted)


def steps(
    image_tokens,
    lift_weight,
    route_token,
    route_cell,
    slot_counts,
    norm_gain,
    w_query,
    w_key,
    w_value,
    w_out,
    key_bias,
):
    n_y = lax.axis_size("bevy")
    n_x = lax.axis_size("bevx")
    slot_count = route_token.shape[3]
    tokens = image_tokens.shape[0]
    width = lift_weight.shape[1]
    head_count = key_bias.shape[2]
    grid_rows = key_bias.shape[0]
    own_cells = ROWS_DEV * COLS_DEV
    edge = HALO * COLS_DEV
    ext = own_cells + edge
    row = lax.axis_index("bevy")
    col = lax.axis_index("bevx")
    core = lax.axis_index("cam")
    up = [(i, (i + 1) % n_x) for i in range(n_x)]
    down = [(b, a) for a, b in up]
    swap = [(0, 1), (1, 0)]
    at = jnp.stack([col, core * edge]).astype(jnp.int32)

    def shift(value, perm):
        return lax.ppermute(value, "bevx", perm)

    u1 = shift(image_tokens, up)
    d1 = shift(image_tokens, down)

    def by_column(value):
        return value.reshape(n_y, n_x, slot_count).transpose(1, 0, 2).reshape(n_x, -1)

    slot = lax.broadcasted_iota(jnp.int32, route_token.shape, 3)
    route = by_column(jnp.where(slot < slot_counts[..., None], route_token, -1))
    cells = by_column(route_cell[:, 0, 0, :])
    cells_other = lax.ppermute(cells, "cam", swap)
    route = lax.all_to_all(route, "bevx", split_axis=0, concat_axis=0, tiled=True)

    u2 = shift(u1, up)
    d2 = shift(d1, down)
    u3 = shift(u2, up)
    d3 = shift(d2, down)
    half = tokens // 2
    u4 = shift(u3[:half], up)
    d4 = shift(d3[half:], down)

    def exchange(rows):
        got = lax.all_to_all(rows, "bevy", split_axis=0, concat_axis=0, tiled=True)
        return got, lax.ppermute(got, "cam", swap)

    def picked(offsets, blocks, extra=()):
        rows = pick(offsets, n_x, n_y, at, route, blocks)
        rows, extra = lax.optimization_barrier((rows, extra))
        return *exchange(rows), extra

    def more(offsets, lifted, pairs):
        [lifted] = local_call(
            lambda *refs: next_sum_kernel(offsets, n_x, *refs),
            (at, pltpu.with_memory_space_constraint(lifted, pltpu.HBM), *pairs, lift_weight),
            [total],
            [pltpu.SemaphoreType.DMA],
            (1,),
        )
        return lifted

    total = jax.ShapeDtypeStruct((ext, width), jnp.float32)
    one, one_other, _ = picked(ONE, (image_tokens, u1, d1))
    two, two_other, _ = picked(TWO, (u2, d2))
    [lifted] = local_call(
        lambda *refs: start_sum_kernel(n_x, *refs),
        (at, one, cells, one_other, cells_other, lift_weight),
        [total],
    )
    near_row = (row * 2 + core) * ROWS_DEV - core * HALO
    far_row = (row * 2 + core) * ROWS_DEV + jnp.where(core == 0, -HALO, ROWS_DEV)
    far_ok = (far_row >= 0) & (far_row < grid_rows)
    near_bias = lax.dynamic_slice_in_dim(key_bias, near_row, ROWS_DEV + HALO, 0)
    far_bias = lax.dynamic_slice_in_dim(
        key_bias, jnp.clip(far_row, 0, grid_rows - HALO), HALO, 0
    )
    far_bias = jnp.where(far_ok, far_bias, jnp.asarray(MASKED, jnp.bfloat16))
    bias = jnp.concatenate([near_bias, far_bias], axis=0).reshape(-1, head_count)
    bias = jnp.pad(bias, ((0, 0), (0, 1)), constant_values=1)
    bias = jnp.pad(bias, ((0, 0), (0, 127 - head_count)))
    late, late_other, bias = picked(LATE, (u3, d3, u4, d4), bias)
    lifted = more(TWO, lifted, (two, cells, two_other, cells_other))
    lifted = more(LATE, lifted, (late, cells))
    own_lifted, normed, sent = local_call(
        lambda *refs: last_sum_kernel(n_x, edge, *refs),
        (at, lifted, late_other, cells_other, lift_weight, norm_gain.reshape(1, -1)),
        [
            jax.ShapeDtypeStruct((own_cells, width), jnp.float32),
            jax.ShapeDtypeStruct((ext, width), jnp.bfloat16),
            jax.ShapeDtypeStruct((edge, width), jnp.bfloat16),
        ],
        [pltpu.VMEM((ext, width), jnp.float32)],
    )
    hops = [(2 * i, 2 * i - 1) for i in range(1, n_y)] + [
        (2 * i + 1, 2 * i + 2) for i in range(n_y - 1)
    ]
    far = lax.ppermute(sent, ("bevy", "cam"), hops)
    queries, keys, values = project(at, normed, w_query, w_key, w_value, own_cells)

    out = attention(
        queries, keys, values, far, w_key, w_value, bias, w_out, own_lifted
    )
    return out.reshape(ROWS_DEV, COLS_DEV, width)


def solution(mesh):
    placed = (
        P(("bevy", "bevx", "cam"), None),
        P(),
        P(("bevy", "bevx"), "cam", None, None),
        P(None, "cam", ("bevy", "bevx"), None),
        P(("bevy", "bevx"), "cam", None),
        P(),
        P(),
        P(),
        P(),
        P(),
        P(None, "bevx", None),
    )
    return jax.shard_map(
        steps,
        mesh=mesh,
        in_specs=placed,
        out_specs=P(("bevy", "cam"), "bevx", None),
        check_vma=False,
    )
```

```python
import jax
import jax.numpy as jnp
from jax import lax
from jax.experimental import pallas as pl
from jax.experimental.pallas import tpu as pltpu
from jax.sharding import PartitionSpec as P


ROWS_DEV = 8
COLS_DEV = 64
HALO = 4
MASKED = -1e30
HEAD_LANES = 16
EARLY = (0, -1, 1, -2, 2)
LATE = (-3, 3, 4)


SCALAR = pl.BlockSpec(memory_space=pltpu.SMEM)
LOCAL = pl.BlockSpec(memory_space=pltpu.VMEM)


def pick_kernel(offsets, n_x, at_ref, route_ref, *refs):
    blocks, out_ref = refs[:-1], refs[-1]
    used = 0
    for i, offset in enumerate(offsets):
        parts = 2
        line = (at_ref[0] + (offset + n_x)) % n_x
        index = route_ref[pl.ds(line, 1), :]
        base = 0
        rows = None
        for block in blocks[used : used + parts]:
            ids = lax.broadcasted_iota(jnp.int32, (block.shape[0], index.shape[1]), 0) + base
            one_hot = jnp.where(ids == index, 1.0, 0.0).astype(jnp.bfloat16)
            got = lax.dot_general(
                one_hot,
                block[...],
                (((0,), (0,)), ((), ())),
                preferred_element_type=jnp.float32,
            )
            rows = got if rows is None else rows + got
            base += block.shape[0]
        used += parts
        out_ref[:, i] = rows.reshape(out_ref.shape[0], out_ref.shape[2], out_ref.shape[3]).astype(
            jnp.bfloat16
        )


def pick(offsets, n_x, n_y, at, route, blocks):
    slots = route.shape[1] // n_y
    width = blocks[0].shape[1]
    return pl.pallas_call(
        lambda *refs: pick_kernel(offsets, n_x, *refs),
        in_specs=[SCALAR] + [LOCAL] * (1 + len(blocks)),
        out_specs=LOCAL,
        out_shape=jax.ShapeDtypeStruct((n_y, len(offsets), slots, width), jnp.bfloat16),
        compiler_params=pltpu.CompilerParams(vmem_limit_bytes=10 << 20),
        name="pick_rows",
    )(at, route, *blocks)


def summed(offsets, n_x, at_ref, pairs, w_ref, total, ready=None):
    for rows_ref, cell_ref in pairs:
        pieces = []
        hots = []
        for i, offset in enumerate(offsets):
            line = (at_ref[0] + (offset + n_x)) % n_x
            cell = cell_ref[pl.ds(line, 1), :]
            piece = rows_ref[:, i]
            pieces.append(piece.reshape(-1, piece.shape[-1]))
            ids = lax.broadcasted_iota(jnp.int32, (total.shape[0], cell.shape[1]), 0) + at_ref[1]
            hots.append(jnp.where(ids == cell, 1.0, 0.0).astype(jnp.bfloat16))
        projected = jnp.dot(
            jnp.concatenate(pieces, axis=0), w_ref[...], preferred_element_type=jnp.float32
        ).astype(jnp.bfloat16)
        added = jnp.dot(
            jnp.concatenate(hots, axis=1), projected, preferred_element_type=jnp.float32
        )
        if ready is not None:
            ready()
        total[...] += added


def first_sum_kernel(n_x, at_ref, a_ref, ac_ref, w_ref, out_ref):
    out_ref[...] = jnp.zeros_like(out_ref)
    summed(EARLY, n_x, at_ref, ((a_ref, ac_ref),), w_ref, out_ref)


def second_sum_kernel(n_x, at_ref, total_ref, a_ref, ac_ref, w_ref, out_ref):
    out_ref[...] = total_ref[...]
    summed(EARLY, n_x, at_ref, ((a_ref, ac_ref),), w_ref, out_ref)


def next_sum_kernel(n_x, at_ref, total_ref, a_ref, ac_ref, w_ref, out_ref, sem):
    copy = pltpu.make_async_copy(total_ref, out_ref, sem)
    copy.start()
    summed(LATE, n_x, at_ref, ((a_ref, ac_ref),), w_ref, out_ref, copy.wait)


def last_sum_kernel(
    n_x, edge, at_ref, total_ref, a_ref, ac_ref, w_ref, gain_ref, own_ref, normed_ref, sent_ref, acc
):
    acc[...] = total_ref[...]
    summed(LATE, n_x, at_ref, ((a_ref, ac_ref),), w_ref, acc)
    rows = own_ref.shape[0]
    own_ref[...] = acc[pl.ds(pl.multiple_of(at_ref[1], edge), rows), :]
    for start in range(0, acc.shape[0], edge):
        lifted = acc[start : start + edge]
        mean_square = jnp.mean(lifted * lifted, axis=-1, keepdims=True)
        normed_ref[start : start + edge] = (
            lifted * lax.rsqrt(mean_square + 1e-06) * gain_ref[...]
        ).astype(jnp.bfloat16)
    sent_ref[...] = normed_ref[pl.ds(pl.multiple_of(2 * at_ref[1], edge), edge), :]


def local_call(kernel, operands, outs, scratch=(), remote=()):
    return pl.pallas_call(
        kernel,
        in_specs=[SCALAR]
        + [
            pl.BlockSpec(memory_space=pltpu.HBM) if i in remote else LOCAL
            for i in range(1, len(operands))
        ],
        out_specs=[LOCAL] * len(outs),
        out_shape=outs,
        scratch_shapes=scratch,
        compiler_params=pltpu.CompilerParams(vmem_limit_bytes=16 << 20),
    )(*operands)


def flipped(w, x):
    return jnp.dot(x, w, preferred_element_type=jnp.float32).T


def project_kernel(at_ref, x_ref, wq_ref, wk_ref, wv_ref, q_ref, k_ref, v_ref):
    rows = q_ref.shape[0]
    own = x_ref[pl.ds(pl.multiple_of(at_ref[1], rows // 2), rows), :]
    x = x_ref[...]
    q_ref[...] = (jnp.dot(own, wq_ref[...], preferred_element_type=jnp.float32)).astype(
        jnp.bfloat16
    )
    k_ref[...] = jnp.dot(x, wk_ref[...], preferred_element_type=jnp.float32).astype(jnp.bfloat16)
    v_ref[...] = flipped(wv_ref[...], x).astype(jnp.bfloat16)


def project(at, x, w_query, w_key, w_value, rows):
    ext, width = x.shape
    return pl.pallas_call(
        project_kernel,
        in_specs=[SCALAR] + [LOCAL] * 4,
        out_specs=[LOCAL] * 3,
        out_shape=[
            jax.ShapeDtypeStruct(shape, jnp.bfloat16)
            for shape in ((rows, width), (ext, width), (width, ext))
        ],
        compiler_params=pltpu.CompilerParams(vmem_limit_bytes=24 << 20),
        name="near_projections",
    )(at, x, w_query, w_key, w_value)


def attention_kernel(
    q_ref, k_ref, v_ref, far_ref, wk_ref, wv_ref, bias_ref, wo_ref, lifted_ref, out_ref, att_ref,
    far_k_ref, far_v_ref,
):
    step = pl.program_id(0)
    rows_q = q_ref.shape[0]
    size = 64
    heads = att_ref.shape[1] // size
    here = pl.ds(pl.multiple_of(step * att_ref.shape[1], 256), att_ref.shape[1])
    q_ref = q_ref.at[:, here]
    k_ref = k_ref.at[:, here]
    v_ref = v_ref.at[here, :]
    wk_ref = wk_ref.at[:, here]
    wv_ref = wv_ref.at[:, here]
    far = far_ref[...]
    far_k_ref[...] = jnp.dot(far, wk_ref[...], preferred_element_type=jnp.float32).astype(
        jnp.bfloat16
    )
    far_v_ref[...] = flipped(wv_ref[...], far).astype(jnp.bfloat16)
    lane = lax.broadcasted_iota(jnp.int32, (rows_q, 128), 1)
    tops = jnp.max(bias_ref[...].astype(jnp.float32), axis=0, keepdims=True)
    lane_top = lax.broadcasted_iota(jnp.int32, tops.shape, 1)

    def scored(head, pair, side):
        cut = pl.ds(pair * 128, 128)
        k = jnp.concatenate([k_ref[:, cut], far_k_ref[:, cut]], axis=0)
        keys = jnp.concatenate([k, bias_ref[...]], axis=1)
        q = q_ref[:, cut] * jnp.asarray(0.125, jnp.bfloat16)
        mine = (lane // size) == side
        number = heads * step + head
        top = jnp.max(jnp.where(lane_top == number, tops, -jnp.inf), axis=1, keepdims=True)
        extra = jnp.where(lane == number, 1.0, jnp.where(lane == HEAD_LANES, -top, 0.0))
        query = jnp.concatenate(
            [jnp.where(mine, q, jnp.zeros((), jnp.bfloat16)), extra.astype(jnp.bfloat16)],
            axis=1,
        )
        return lax.dot_general(
            keys, query, (((1,), (1,)), ((), ())), preferred_element_type=jnp.float32
        )

    def weighed(own, weight):
        v = jnp.concatenate([v_ref[own, :], far_v_ref[own, :]], axis=1)
        values = jnp.concatenate([v, jnp.ones((16, v.shape[1]), jnp.bfloat16)], axis=0)
        mixed = jnp.dot(values, weight, preferred_element_type=jnp.float32)
        total = mixed[size : size + 1]
        att_ref[step, own, :] = (mixed[:size] / total).astype(jnp.bfloat16)
        return total

    least = most = None
    scores = [scored(0, 0, 0)]
    for head in range(heads):
        if head + 1 < heads:
            scores.append(scored(head + 1, (head + 1) // 2, (head + 1) % 2))
        total = weighed(
            slice(head * size, head * size + size), jnp.exp(scores[head]).astype(jnp.bfloat16)
        )
        least = total if head == 0 else jnp.minimum(least, total)
        most = total if head == 0 else jnp.maximum(most, total)
    safe = (jnp.min(least) > 1e-18) & (jnp.max(most) < 1e30)

    @pl.when(jnp.logical_not(safe))
    def _():
        def again(head, carry):
            score = scored(head, head // 2, head % 2)
            weight = jnp.exp(score - jnp.max(score, axis=0, keepdims=True)).astype(jnp.bfloat16)
            weighed(pl.ds(pl.multiple_of(head * size, size), size), weight)
            return carry

        lax.fori_loop(0, heads, again, 0)

    @pl.when(step == pl.num_programs(0) - 1)
    def _():
        attended = att_ref[...].reshape(-1, rows_q)
        mixed = lax.dot_general(
            attended, wo_ref[...], (((0,), (0,)), ((), ())), preferred_element_type=jnp.float32
        )
        out_ref[...] = (lifted_ref[...] + mixed).astype(jnp.bfloat16)


def attention(q, k, v, far, w_key, w_value, bias, w_out, lifted):
    rows, width = q.shape
    block = 256
    return pl.pallas_call(
        attention_kernel,
        grid=(width // block,),
        in_specs=[LOCAL] * 9,
        out_specs=LOCAL,
        out_shape=jax.ShapeDtypeStruct((rows, width), jnp.bfloat16),
        scratch_shapes=[
            pltpu.VMEM((width // block, block, rows), jnp.bfloat16),
            pltpu.VMEM((far.shape[0], block), jnp.bfloat16),
            pltpu.VMEM((block, far.shape[0]), jnp.bfloat16),
        ],
        compiler_params=pltpu.CompilerParams(
            dimension_semantics=("arbitrary",), vmem_limit_bytes=28 << 20
        ),
        name="window_attention",
    )(q, k, v, far, w_key, w_value, bias, w_out, lifted)


def steps(
    image_tokens,
    lift_weight,
    route_token,
    route_cell,
    slot_counts,
    norm_gain,
    w_query,
    w_key,
    w_value,
    w_out,
    key_bias,
):
    n_y = lax.axis_size("bevy")
    n_x = lax.axis_size("bevx")
    slot_count = route_token.shape[3]
    tokens = image_tokens.shape[0]
    width = lift_weight.shape[1]
    head_count = key_bias.shape[2]
    grid_rows = key_bias.shape[0]
    own_cells = ROWS_DEV * COLS_DEV
    edge = HALO * COLS_DEV
    ext = own_cells + edge
    row = lax.axis_index("bevy")
    col = lax.axis_index("bevx")
    core = lax.axis_index("cam")
    up = [(i, (i + 1) % n_x) for i in range(n_x)]
    down = [(b, a) for a, b in up]
    swap = [(0, 1), (1, 0)]
    at = jnp.stack([col, core * edge]).astype(jnp.int32)

    half = tokens // 2
    own = [image_tokens[:half], image_tokens[half:]]

    def shift(values, perm, pieces=(0, 1)):
        moved = []
        for piece in pieces:
            moved.append(lax.ppermute(values[piece], "bevx", perm))
        return moved

    u1 = shift(own, up)
    d1 = shift(own, down)

    def by_column(value):
        return value.reshape(n_y, n_x, slot_count).transpose(1, 0, 2).reshape(n_x, -1)

    slot = lax.broadcasted_iota(jnp.int32, route_token.shape, 3)
    route = by_column(jnp.where(slot < slot_counts[..., None], route_token, -1))
    cells = by_column(route_cell[:, 0, 0, :])
    cells_other = lax.ppermute(cells, "cam", swap)
    route = lax.all_to_all(route, "bevx", split_axis=0, concat_axis=0, tiled=True)

    u2 = shift(u1, up)
    d2 = shift(d1, down)
    u3 = shift(u2, up)
    d3 = shift(d2, down)
    u4 = shift(u3, up, (0,))
    d4 = shift(d3, down, (1,))

    near_row = (row * 2 + core) * ROWS_DEV - core * HALO
    far_row = (row * 2 + core) * ROWS_DEV + jnp.where(core == 0, -HALO, ROWS_DEV)
    far_ok = (far_row >= 0) & (far_row < grid_rows)
    near_bias = lax.dynamic_slice_in_dim(key_bias, near_row, ROWS_DEV + HALO, 0)
    far_bias = lax.dynamic_slice_in_dim(key_bias, jnp.clip(far_row, 0, grid_rows - HALO), HALO, 0)
    far_bias = jnp.where(far_ok, far_bias, jnp.asarray(MASKED, jnp.bfloat16))
    bias = jnp.concatenate([near_bias, far_bias], axis=0).reshape(-1, head_count)
    bias = jnp.pad(bias, ((0, 0), (0, 1)), constant_values=1)
    bias = jnp.pad(bias, ((0, 0), (0, 127 - head_count)))

    def exchange(rows):
        got = lax.all_to_all(rows, "bevy", split_axis=0, concat_axis=0, tiled=True)
        return got, lax.ppermute(got, "cam", swap)

    rows = pick(EARLY, n_x, n_y, at, route, (*own, *u1, *d1, *u2, *d2))
    rows, bias, cells_other = lax.optimization_barrier((rows, bias, cells_other))
    early, early_other = exchange(rows)
    total = jax.ShapeDtypeStruct((ext, width), jnp.float32)
    [lifted] = local_call(
        lambda *refs: first_sum_kernel(n_x, *refs), (at, early, cells, lift_weight), [total]
    )
    [lifted] = local_call(
        lambda *refs: second_sum_kernel(n_x, *refs),
        (at, lifted, early_other, cells_other, lift_weight),
        [total],
    )
    rows = pick(LATE, n_x, n_y, at, route, (*u3, *d3, *u4, *d4))
    late, late_other = exchange(rows)
    [lifted] = local_call(
        lambda *refs: next_sum_kernel(n_x, *refs),
        (
            at,
            pltpu.with_memory_space_constraint(lifted, pltpu.HBM),
            late,
            cells,
            lift_weight,
        ),
        [total],
        [pltpu.SemaphoreType.DMA],
        (1,),
    )
    own_lifted, normed, sent = local_call(
        lambda *refs: last_sum_kernel(n_x, edge, *refs),
        (at, lifted, late_other, cells_other, lift_weight, norm_gain.reshape(1, -1)),
        [
            jax.ShapeDtypeStruct((own_cells, width), jnp.float32),
            jax.ShapeDtypeStruct((ext, width), jnp.bfloat16),
            jax.ShapeDtypeStruct((edge, width), jnp.bfloat16),
        ],
        [pltpu.VMEM((ext, width), jnp.float32)],
    )
    hops = [(2 * i, 2 * i - 1) for i in range(1, n_y)] + [
        (2 * i + 1, 2 * i + 2) for i in range(n_y - 1)
    ]
    far = lax.ppermute(sent, ("bevy", "cam"), hops)
    queries, keys, values = project(at, normed, w_query, w_key, w_value, own_cells)

    out = attention(
        queries, keys, values, far, w_key, w_value, bias, w_out, own_lifted
    )
    return out.reshape(ROWS_DEV, COLS_DEV, width)


def solution(mesh):
    placed = (
        P(("bevy", "bevx", "cam"), None),
        P(),
        P(("bevy", "bevx"), "cam", None, None),
        P(None, "cam", ("bevy", "bevx"), None),
        P(("bevy", "bevx"), "cam", None),
        P(),
        P(),
        P(),
        P(),
        P(),
        P(None, "bevx", None),
    )
    return jax.shard_map(
        steps,
        mesh=mesh,
        in_specs=placed,
        out_specs=P(("bevy", "cam"), "bevx", None),
        check_vma=False,
    )
```

```python
import jax
import jax.numpy as jnp
from jax import lax
from jax.experimental import pallas as pl
from jax.experimental.pallas import tpu as pltpu
from jax.sharding import PartitionSpec as P


ROWS_DEV = 8
COLS_DEV = 64
HALO = 4
MASKED = -1e30
HEAD_LANES = 16
EARLY = (0, -1, 1, -2, 2)
LATE = (-3, 3, 4)


SCALAR = pl.BlockSpec(memory_space=pltpu.SMEM)
LOCAL = pl.BlockSpec(memory_space=pltpu.VMEM)


def pick_kernel(offsets, n_x, at_ref, route_ref, *refs):
    blocks, out_ref = refs[:-1], refs[-1]
    lines = [(at_ref[0] + (offset + n_x)) % n_x for offset in offsets]
    lines += lines[:1] * (8 - len(lines))
    index = jnp.concatenate([route_ref[pl.ds(line, 1), :] for line in lines], axis=0).T
    for i in range(len(offsets)):
        rows = None
        base = 0
        for block in blocks[2 * i : 2 * i + 2]:
            ids = lax.broadcasted_iota(jnp.int32, (index.shape[0], block.shape[0]), 1) + base
            one_hot = jnp.where(ids == index[:, i : i + 1], 1.0, 0.0).astype(jnp.bfloat16)
            got = jnp.dot(one_hot, block[...], preferred_element_type=jnp.float32)
            rows = got if rows is None else rows + got
            base += block.shape[0]
        out_ref[:, i] = rows.reshape(out_ref.shape[0], out_ref.shape[2], out_ref.shape[3]).astype(
            jnp.bfloat16
        )


def pick(offsets, n_x, n_y, at, route, blocks):
    slots = route.shape[1] // n_y
    width = blocks[0].shape[1]
    return pl.pallas_call(
        lambda *refs: pick_kernel(offsets, n_x, *refs),
        in_specs=[SCALAR] + [LOCAL] * (1 + len(blocks)),
        out_specs=LOCAL,
        out_shape=jax.ShapeDtypeStruct((n_y, len(offsets), slots, width), jnp.bfloat16),
        compiler_params=pltpu.CompilerParams(vmem_limit_bytes=10 << 20),
        name="pick_rows",
    )(at, route, *blocks)


def summed(offsets, n_x, at_ref, pairs, w_ref, total, ready=None):
    for rows_ref, cell_ref in pairs:
        pieces = []
        hots = []
        for i, offset in enumerate(offsets):
            line = (at_ref[0] + (offset + n_x)) % n_x
            cell = cell_ref[pl.ds(line, 1), :]
            piece = rows_ref[:, i]
            pieces.append(piece.reshape(-1, piece.shape[-1]))
            ids = lax.broadcasted_iota(jnp.int32, (total.shape[0], cell.shape[1]), 0) + at_ref[1]
            hots.append(jnp.where(ids == cell, 1.0, 0.0).astype(jnp.bfloat16))
        projected = jnp.dot(
            jnp.concatenate(pieces, axis=0), w_ref[...], preferred_element_type=jnp.float32
        ).astype(jnp.bfloat16)
        if ready is not None:
            ready()
        total[...] += jnp.dot(
            jnp.concatenate(hots, axis=1), projected, preferred_element_type=jnp.float32
        )


def first_sum_kernel(n_x, at_ref, a_ref, ac_ref, w_ref, out_ref):
    out_ref[...] = jnp.zeros_like(out_ref)
    summed(EARLY, n_x, at_ref, ((a_ref, ac_ref),), w_ref, out_ref)


def second_sum_kernel(n_x, at_ref, total_ref, a_ref, ac_ref, w_ref, out_ref):
    out_ref[...] = total_ref[...]
    summed(EARLY, n_x, at_ref, ((a_ref, ac_ref),), w_ref, out_ref)


def next_sum_kernel(n_x, at_ref, total_ref, a_ref, ac_ref, w_ref, out_ref, sem):
    copy = pltpu.make_async_copy(total_ref, out_ref, sem)
    copy.start()
    summed(LATE, n_x, at_ref, ((a_ref, ac_ref),), w_ref, out_ref, copy.wait)


def last_sum_kernel(
    n_x, edge, at_ref, total_ref, a_ref, ac_ref, w_ref, gain_ref, own_ref, normed_ref, sent_ref, acc
):
    acc[...] = total_ref[...]
    summed(LATE, n_x, at_ref, ((a_ref, ac_ref),), w_ref, acc)
    rows = own_ref.shape[0]
    own_ref[...] = acc[pl.ds(pl.multiple_of(at_ref[1], edge), rows), :]
    for start in range(0, acc.shape[0], edge):
        lifted = acc[start : start + edge]
        mean_square = jnp.mean(lifted * lifted, axis=-1, keepdims=True)
        normed_ref[start : start + edge] = (
            lifted * lax.rsqrt(mean_square + 1e-06) * gain_ref[...]
        ).astype(jnp.bfloat16)
    sent_ref[...] = normed_ref[pl.ds(pl.multiple_of(2 * at_ref[1], edge), edge), :]


def local_call(kernel, operands, outs, scratch=(), remote=()):
    return pl.pallas_call(
        kernel,
        in_specs=[SCALAR]
        + [
            pl.BlockSpec(memory_space=pltpu.HBM) if i in remote else LOCAL
            for i in range(1, len(operands))
        ],
        out_specs=[LOCAL] * len(outs),
        out_shape=outs,
        scratch_shapes=scratch,
        compiler_params=pltpu.CompilerParams(vmem_limit_bytes=16 << 20),
    )(*operands)


def flipped(w, x):
    return jnp.dot(x, w, preferred_element_type=jnp.float32).T


def project_kernel(at_ref, x_ref, wq_ref, wk_ref, wv_ref, q_ref, k_ref, v_ref):
    rows = q_ref.shape[0]
    own = x_ref[pl.ds(pl.multiple_of(at_ref[1], rows // 2), rows), :]
    x = x_ref[...]
    q_ref[...] = (jnp.dot(own, wq_ref[...], preferred_element_type=jnp.float32)).astype(
        jnp.bfloat16
    )
    k_ref[...] = jnp.dot(x, wk_ref[...], preferred_element_type=jnp.float32).astype(jnp.bfloat16)
    v_ref[...] = flipped(wv_ref[...], x).astype(jnp.bfloat16)


def project(at, x, w_query, w_key, w_value, rows):
    ext, width = x.shape
    return pl.pallas_call(
        project_kernel,
        in_specs=[SCALAR] + [LOCAL] * 4,
        out_specs=[LOCAL] * 3,
        out_shape=[
            jax.ShapeDtypeStruct(shape, jnp.bfloat16)
            for shape in ((rows, width), (ext, width), (width, ext))
        ],
        compiler_params=pltpu.CompilerParams(vmem_limit_bytes=24 << 20),
        name="near_projections",
    )(at, x, w_query, w_key, w_value)


def attention_kernel(
    q_ref, k_ref, v_ref, far_ref, wk_ref, wv_ref, bias_ref, wo_ref, lifted_ref, out_ref, att_ref,
    far_k_ref, far_v_ref,
):
    step = pl.program_id(0)
    rows_q = q_ref.shape[0]
    size = 64
    heads = att_ref.shape[1] // size
    here = pl.ds(pl.multiple_of(step * att_ref.shape[1], 256), att_ref.shape[1])
    q_ref = q_ref.at[:, here]
    k_ref = k_ref.at[:, here]
    v_ref = v_ref.at[here, :]
    wk_ref = wk_ref.at[:, here]
    wv_ref = wv_ref.at[:, here]
    far = far_ref[...]
    far_k_ref[...] = jnp.dot(far, wk_ref[...], preferred_element_type=jnp.float32).astype(
        jnp.bfloat16
    )
    far_v_ref[...] = flipped(wv_ref[...], far).astype(jnp.bfloat16)
    lane = lax.broadcasted_iota(jnp.int32, (rows_q, 128), 1)
    tops = jnp.max(bias_ref[...].astype(jnp.float32), axis=0, keepdims=True)
    lane_top = lax.broadcasted_iota(jnp.int32, tops.shape, 1)

    def scored(head, pair, side):
        cut = pl.ds(pair * 128, 128)
        k = jnp.concatenate([k_ref[:, cut], far_k_ref[:, cut]], axis=0)
        keys = jnp.concatenate([k, bias_ref[...]], axis=1)
        q = q_ref[:, cut] * jnp.asarray(0.125, jnp.bfloat16)
        mine = (lane // size) == side
        number = heads * step + head
        top = jnp.max(jnp.where(lane_top == number, tops, -jnp.inf), axis=1, keepdims=True)
        extra = jnp.where(lane == number, 1.0, jnp.where(lane == HEAD_LANES, -top, 0.0))
        query = jnp.concatenate(
            [jnp.where(mine, q, jnp.zeros((), jnp.bfloat16)), extra.astype(jnp.bfloat16)],
            axis=1,
        )
        return lax.dot_general(
            keys, query, (((1,), (1,)), ((), ())), preferred_element_type=jnp.float32
        )

    def weighed(own, weight):
        v = jnp.concatenate([v_ref[own, :], far_v_ref[own, :]], axis=1)
        values = jnp.concatenate([v, jnp.ones((16, v.shape[1]), jnp.bfloat16)], axis=0)
        mixed = jnp.dot(values, weight, preferred_element_type=jnp.float32)
        total = mixed[size : size + 1]
        att_ref[step, own, :] = (mixed[:size] / total).astype(jnp.bfloat16)
        return total

    least = most = None
    scores = [scored(0, 0, 0)]
    for head in range(heads):
        if head + 1 < heads:
            scores.append(scored(head + 1, (head + 1) // 2, (head + 1) % 2))
        total = weighed(
            slice(head * size, head * size + size), jnp.exp(scores[head]).astype(jnp.bfloat16)
        )
        least = total if head == 0 else jnp.minimum(least, total)
        most = total if head == 0 else jnp.maximum(most, total)
    safe = (jnp.min(least) > 1e-18) & (jnp.max(most) < 1e30)

    @pl.when(jnp.logical_not(safe))
    def _():
        def again(head, carry):
            score = scored(head, head // 2, head % 2)
            weight = jnp.exp(score - jnp.max(score, axis=0, keepdims=True)).astype(jnp.bfloat16)
            weighed(pl.ds(pl.multiple_of(head * size, size), size), weight)
            return carry

        lax.fori_loop(0, heads, again, 0)

    @pl.when(step == pl.num_programs(0) - 1)
    def _():
        attended = att_ref[...].reshape(-1, rows_q)
        mixed = lax.dot_general(
            attended, wo_ref[...], (((0,), (0,)), ((), ())), preferred_element_type=jnp.float32
        )
        out_ref[...] = (lifted_ref[...] + mixed).astype(jnp.bfloat16)


def attention(q, k, v, far, w_key, w_value, bias, w_out, lifted):
    rows, width = q.shape
    block = 256
    return pl.pallas_call(
        attention_kernel,
        grid=(width // block,),
        in_specs=[LOCAL] * 9,
        out_specs=LOCAL,
        out_shape=jax.ShapeDtypeStruct((rows, width), jnp.bfloat16),
        scratch_shapes=[
            pltpu.VMEM((width // block, block, rows), jnp.bfloat16),
            pltpu.VMEM((far.shape[0], block), jnp.bfloat16),
            pltpu.VMEM((block, far.shape[0]), jnp.bfloat16),
        ],
        compiler_params=pltpu.CompilerParams(
            dimension_semantics=("arbitrary",), vmem_limit_bytes=28 << 20
        ),
        name="window_attention",
    )(q, k, v, far, w_key, w_value, bias, w_out, lifted)


def steps(
    image_tokens,
    lift_weight,
    route_token,
    route_cell,
    slot_counts,
    norm_gain,
    w_query,
    w_key,
    w_value,
    w_out,
    key_bias,
):
    n_y = lax.axis_size("bevy")
    n_x = lax.axis_size("bevx")
    slot_count = route_token.shape[3]
    tokens = image_tokens.shape[0]
    width = lift_weight.shape[1]
    head_count = key_bias.shape[2]
    grid_rows = key_bias.shape[0]
    own_cells = ROWS_DEV * COLS_DEV
    edge = HALO * COLS_DEV
    ext = own_cells + edge
    row = lax.axis_index("bevy")
    col = lax.axis_index("bevx")
    core = lax.axis_index("cam")
    up = [(i, (i + 1) % n_x) for i in range(n_x)]
    down = [(b, a) for a, b in up]
    swap = [(0, 1), (1, 0)]
    at = jnp.stack([col, core * edge]).astype(jnp.int32)

    half = tokens // 2
    own = [image_tokens[:half], image_tokens[half:]]

    def shift(values, perm, pieces=(0, 1)):
        moved = []
        for piece in pieces:
            moved.append(lax.ppermute(values[piece], "bevx", perm))
        return moved

    u1 = shift(own, up)
    d1 = shift(own, down)

    def by_column(value):
        return value.reshape(n_y, n_x, slot_count).transpose(1, 0, 2).reshape(n_x, -1)

    slot = lax.broadcasted_iota(jnp.int32, route_token.shape, 3)
    route = by_column(jnp.where(slot < slot_counts[..., None], route_token, -1))
    cells = by_column(route_cell[:, 0, 0, :])
    cells_other = lax.ppermute(cells, "cam", swap)
    route = lax.all_to_all(route, "bevx", split_axis=0, concat_axis=0, tiled=True)

    u2 = shift(u1, up)
    d2 = shift(d1, down)
    u3 = shift(u2, up)
    d3 = shift(d2, down)
    u4 = shift(u3, up, (0,))
    d4 = shift(d3, down, (1,))

    near_row = (row * 2 + core) * ROWS_DEV - core * HALO
    far_row = (row * 2 + core) * ROWS_DEV + jnp.where(core == 0, -HALO, ROWS_DEV)
    far_ok = (far_row >= 0) & (far_row < grid_rows)
    near_bias = lax.dynamic_slice_in_dim(key_bias, near_row, ROWS_DEV + HALO, 0)
    far_bias = lax.dynamic_slice_in_dim(key_bias, jnp.clip(far_row, 0, grid_rows - HALO), HALO, 0)
    far_bias = jnp.where(far_ok, far_bias, jnp.asarray(MASKED, jnp.bfloat16))
    bias = jnp.concatenate([near_bias, far_bias], axis=0).reshape(-1, head_count)
    bias = jnp.pad(bias, ((0, 0), (0, 1)), constant_values=1)
    bias = jnp.pad(bias, ((0, 0), (0, 127 - head_count)))

    def exchange(rows):
        got = lax.all_to_all(rows, "bevy", split_axis=0, concat_axis=0, tiled=True)
        return got, lax.ppermute(got, "cam", swap)

    rows = pick(EARLY, n_x, n_y, at, route, (*own, *u1, *d1, *u2, *d2))
    rows, bias = lax.optimization_barrier((rows, bias))
    early, early_other = exchange(rows)
    total = jax.ShapeDtypeStruct((ext, width), jnp.float32)
    [lifted] = local_call(
        lambda *refs: first_sum_kernel(n_x, *refs), (at, early, cells, lift_weight), [total]
    )
    [lifted] = local_call(
        lambda *refs: second_sum_kernel(n_x, *refs),
        (at, lifted, early_other, cells_other, lift_weight),
        [total],
    )
    rows = pick(LATE, n_x, n_y, at, route, (*u3, *d3, *u4, *d4))
    late, late_other = exchange(rows)
    [lifted] = local_call(
        lambda *refs: next_sum_kernel(n_x, *refs),
        (
            at,
            pltpu.with_memory_space_constraint(lifted, pltpu.HBM),
            late,
            cells,
            lift_weight,
        ),
        [total],
        [pltpu.SemaphoreType.DMA],
        (1,),
    )
    own_lifted, normed, sent = local_call(
        lambda *refs: last_sum_kernel(n_x, edge, *refs),
        (at, lifted, late_other, cells_other, lift_weight, norm_gain.reshape(1, -1)),
        [
            jax.ShapeDtypeStruct((own_cells, width), jnp.float32),
            jax.ShapeDtypeStruct((ext, width), jnp.bfloat16),
            jax.ShapeDtypeStruct((edge, width), jnp.bfloat16),
        ],
        [pltpu.VMEM((ext, width), jnp.float32)],
    )
    hops = [(2 * i, 2 * i - 1) for i in range(1, n_y)] + [
        (2 * i + 1, 2 * i + 2) for i in range(n_y - 1)
    ]
    far = lax.ppermute(sent, ("bevy", "cam"), hops)
    queries, keys, values = project(at, normed, w_query, w_key, w_value, own_cells)

    out = attention(
        queries, keys, values, far, w_key, w_value, bias, w_out, own_lifted
    )
    return out.reshape(ROWS_DEV, COLS_DEV, width)


def solution(mesh):
    placed = (
        P(("bevy", "bevx", "cam"), None),
        P(),
        P(("bevy", "bevx"), "cam", None, None),
        P(None, "cam", ("bevy", "bevx"), None),
        P(("bevy", "bevx"), "cam", None),
        P(),
        P(),
        P(),
        P(),
        P(),
        P(None, "bevx", None),
    )
    return jax.shard_map(
        steps,
        mesh=mesh,
        in_specs=placed,
        out_specs=P(("bevy", "cam"), "bevx", None),
        check_vma=False,
    )
```

```python
import jax
import jax.numpy as jnp
from jax import lax
from jax.experimental import pallas as pl
from jax.experimental.pallas import tpu as pltpu
from jax.sharding import PartitionSpec as P


ROWS_DEV = 8
COLS_DEV = 64
HALO = 4
MASKED = -1e30
HEAD_LANES = 16
EARLY = (0, -1, 1, -2, 2)
LATE = (-3, 3, 4)


SCALAR = pl.BlockSpec(memory_space=pltpu.SMEM)
LOCAL = pl.BlockSpec(memory_space=pltpu.VMEM)


def pick_kernel(offsets, n_x, at_ref, route_ref, *refs):
    blocks, out_ref = refs[:-1], refs[-1]
    used = 0
    for i, offset in enumerate(offsets):
        parts = 2 if offset == n_x // 2 else 1
        line = (at_ref[0] + (offset + n_x)) % n_x
        index = route_ref[pl.ds(line, 1), :]
        base = 0
        rows = None
        for block in blocks[used : used + parts]:
            ids = lax.broadcasted_iota(jnp.int32, (block.shape[0], index.shape[1]), 0) + base
            one_hot = jnp.where(ids == index, 1.0, 0.0).astype(jnp.bfloat16)
            got = lax.dot_general(
                one_hot,
                block[...],
                (((0,), (0,)), ((), ())),
                preferred_element_type=jnp.float32,
            )
            rows = got if rows is None else rows + got
            base += block.shape[0]
        used += parts
        out_ref[:, i] = rows.reshape(out_ref.shape[0], out_ref.shape[2], out_ref.shape[3]).astype(
            jnp.bfloat16
        )


def pick(offsets, n_x, n_y, at, route, blocks):
    slots = route.shape[1] // n_y
    width = blocks[0].shape[1]
    return pl.pallas_call(
        lambda *refs: pick_kernel(offsets, n_x, *refs),
        in_specs=[SCALAR] + [LOCAL] * (1 + len(blocks)),
        out_specs=LOCAL,
        out_shape=jax.ShapeDtypeStruct((n_y, len(offsets), slots, width), jnp.bfloat16),
        compiler_params=pltpu.CompilerParams(vmem_limit_bytes=10 << 20),
        name="pick_rows",
    )(at, route, *blocks)


def cut_kernel(half, a_ref, b_ref, low_ref, high_ref, sems):
    copies = (
        pltpu.make_async_copy(a_ref.at[pl.ds(0, half)], low_ref, sems.at[0]),
        pltpu.make_async_copy(b_ref.at[pl.ds(half, half)], high_ref, sems.at[1]),
    )
    for copy in copies:
        copy.start()
    for copy in copies:
        copy.wait()


def cut(a, b):
    half = a.shape[0] // 2
    piece = jax.ShapeDtypeStruct((half, a.shape[1]), a.dtype)
    return pl.pallas_call(
        lambda *refs: cut_kernel(half, *refs),
        in_specs=[pl.BlockSpec(memory_space=pl.ANY)] * 2,
        out_specs=[LOCAL] * 2,
        out_shape=[piece, piece],
        scratch_shapes=[pltpu.SemaphoreType.DMA((2,))],
        compiler_params=pltpu.CompilerParams(vmem_limit_bytes=2 << 20),
        name="cut_halves",
    )(a, b)


def summed(offsets, n_x, at_ref, pairs, w_ref, total, ready=None):
    for rows_ref, cell_ref in pairs:
        pieces = []
        hots = []
        for i, offset in enumerate(offsets):
            line = (at_ref[0] + (offset + n_x)) % n_x
            cell = cell_ref[pl.ds(line, 1), :]
            piece = rows_ref[:, i]
            pieces.append(piece.reshape(-1, piece.shape[-1]))
            ids = lax.broadcasted_iota(jnp.int32, (total.shape[0], cell.shape[1]), 0) + at_ref[1]
            hots.append(jnp.where(ids == cell, 1.0, 0.0).astype(jnp.bfloat16))
        projected = jnp.dot(
            jnp.concatenate(pieces, axis=0), w_ref[...], preferred_element_type=jnp.float32
        ).astype(jnp.bfloat16)
        added = jnp.dot(
            jnp.concatenate(hots, axis=1), projected, preferred_element_type=jnp.float32
        )
        if ready is not None:
            ready()
        total[...] += added


def first_sum_kernel(n_x, at_ref, a_ref, ac_ref, w_ref, out_ref):
    out_ref[...] = jnp.zeros_like(out_ref)
    summed(EARLY, n_x, at_ref, ((a_ref, ac_ref),), w_ref, out_ref)


def second_sum_kernel(n_x, at_ref, total_ref, a_ref, ac_ref, w_ref, out_ref):
    out_ref[...] = total_ref[...]
    summed(EARLY, n_x, at_ref, ((a_ref, ac_ref),), w_ref, out_ref)


def next_sum_kernel(n_x, at_ref, total_ref, a_ref, ac_ref, w_ref, out_ref, sem):
    copy = pltpu.make_async_copy(total_ref, out_ref, sem)
    copy.start()
    summed(LATE, n_x, at_ref, ((a_ref, ac_ref),), w_ref, out_ref, copy.wait)


def last_sum_kernel(
    n_x, edge, at_ref, total_ref, a_ref, ac_ref, w_ref, gain_ref, own_ref, normed_ref, sent_ref, acc
):
    acc[...] = total_ref[...]
    summed(LATE, n_x, at_ref, ((a_ref, ac_ref),), w_ref, acc)
    rows = own_ref.shape[0]
    own_ref[...] = acc[pl.ds(pl.multiple_of(at_ref[1], edge), rows), :]
    for start in range(0, acc.shape[0], edge):
        lifted = acc[start : start + edge]
        mean_square = jnp.mean(lifted * lifted, axis=-1, keepdims=True)
        normed_ref[start : start + edge] = (
            lifted * lax.rsqrt(mean_square + 1e-06) * gain_ref[...]
        ).astype(jnp.bfloat16)
    sent_ref[...] = normed_ref[pl.ds(pl.multiple_of(2 * at_ref[1], edge), edge), :]


def local_call(kernel, operands, outs, scratch=(), remote=()):
    return pl.pallas_call(
        kernel,
        in_specs=[SCALAR]
        + [
            pl.BlockSpec(memory_space=pltpu.HBM) if i in remote else LOCAL
            for i in range(1, len(operands))
        ],
        out_specs=[LOCAL] * len(outs),
        out_shape=outs,
        scratch_shapes=scratch,
        compiler_params=pltpu.CompilerParams(vmem_limit_bytes=16 << 20),
    )(*operands)


def flipped(w, x):
    return jnp.dot(x, w, preferred_element_type=jnp.float32).T


def project_kernel(at_ref, x_ref, wq_ref, wk_ref, wv_ref, q_ref, k_ref, v_ref):
    rows = q_ref.shape[0]
    own = x_ref[pl.ds(pl.multiple_of(at_ref[1], rows // 2), rows), :]
    x = x_ref[...]
    q_ref[...] = (jnp.dot(own, wq_ref[...], preferred_element_type=jnp.float32)).astype(
        jnp.bfloat16
    )
    k_ref[...] = jnp.dot(x, wk_ref[...], preferred_element_type=jnp.float32).astype(jnp.bfloat16)
    v_ref[...] = flipped(wv_ref[...], x).astype(jnp.bfloat16)


def project(at, x, w_query, w_key, w_value, rows):
    ext, width = x.shape
    return pl.pallas_call(
        project_kernel,
        in_specs=[SCALAR] + [LOCAL] * 4,
        out_specs=[LOCAL] * 3,
        out_shape=[
            jax.ShapeDtypeStruct(shape, jnp.bfloat16)
            for shape in ((rows, width), (ext, width), (width, ext))
        ],
        compiler_params=pltpu.CompilerParams(vmem_limit_bytes=24 << 20),
        name="near_projections",
    )(at, x, w_query, w_key, w_value)


def attention_kernel(
    q_ref, k_ref, v_ref, far_ref, wk_ref, wv_ref, bias_ref, wo_ref, lifted_ref, out_ref, att_ref,
    far_k_ref, far_v_ref,
):
    step = pl.program_id(0)
    rows_q = q_ref.shape[0]
    size = 64
    heads = att_ref.shape[1] // size
    here = pl.ds(pl.multiple_of(step * att_ref.shape[1], 256), att_ref.shape[1])
    q_ref = q_ref.at[:, here]
    k_ref = k_ref.at[:, here]
    v_ref = v_ref.at[here, :]
    wk_ref = wk_ref.at[:, here]
    wv_ref = wv_ref.at[:, here]
    far = far_ref[...]
    far_k_ref[...] = jnp.dot(far, wk_ref[...], preferred_element_type=jnp.float32).astype(
        jnp.bfloat16
    )
    far_v_ref[...] = flipped(wv_ref[...], far).astype(jnp.bfloat16)
    lane = lax.broadcasted_iota(jnp.int32, (rows_q, 128), 1)
    tops = jnp.max(bias_ref[...].astype(jnp.float32), axis=0, keepdims=True)
    lane_top = lax.broadcasted_iota(jnp.int32, tops.shape, 1)

    def scored(head, pair, side):
        cut = pl.ds(pair * 128, 128)
        k = jnp.concatenate([k_ref[:, cut], far_k_ref[:, cut]], axis=0)
        keys = jnp.concatenate([k, bias_ref[...]], axis=1)
        q = q_ref[:, cut] * jnp.asarray(0.125, jnp.bfloat16)
        mine = (lane // size) == side
        number = heads * step + head
        top = jnp.max(jnp.where(lane_top == number, tops, -jnp.inf), axis=1, keepdims=True)
        extra = jnp.where(lane == number, 1.0, jnp.where(lane == HEAD_LANES, -top, 0.0))
        query = jnp.concatenate(
            [jnp.where(mine, q, jnp.zeros((), jnp.bfloat16)), extra.astype(jnp.bfloat16)],
            axis=1,
        )
        return lax.dot_general(
            keys, query, (((1,), (1,)), ((), ())), preferred_element_type=jnp.float32
        )

    def weighed(own, weight):
        v = jnp.concatenate([v_ref[own, :], far_v_ref[own, :]], axis=1)
        values = jnp.concatenate([v, jnp.ones((16, v.shape[1]), jnp.bfloat16)], axis=0)
        mixed = jnp.dot(values, weight, preferred_element_type=jnp.float32)
        total = mixed[size : size + 1]
        att_ref[step, own, :] = (mixed[:size] / total).astype(jnp.bfloat16)
        return total

    least = most = None
    scores = [scored(0, 0, 0)]
    for head in range(heads):
        if head + 1 < heads:
            scores.append(scored(head + 1, (head + 1) // 2, (head + 1) % 2))
        total = weighed(
            slice(head * size, head * size + size), jnp.exp(scores[head]).astype(jnp.bfloat16)
        )
        least = total if head == 0 else jnp.minimum(least, total)
        most = total if head == 0 else jnp.maximum(most, total)
    safe = (jnp.min(least) > 1e-18) & (jnp.max(most) < 1e30)

    @pl.when(jnp.logical_not(safe))
    def _():
        def again(head, carry):
            score = scored(head, head // 2, head % 2)
            weight = jnp.exp(score - jnp.max(score, axis=0, keepdims=True)).astype(jnp.bfloat16)
            weighed(pl.ds(pl.multiple_of(head * size, size), size), weight)
            return carry

        lax.fori_loop(0, heads, again, 0)

    @pl.when(step == pl.num_programs(0) - 1)
    def _():
        attended = att_ref[...].reshape(-1, rows_q)
        mixed = lax.dot_general(
            attended, wo_ref[...], (((0,), (0,)), ((), ())), preferred_element_type=jnp.float32
        )
        out_ref[...] = (lifted_ref[...] + mixed).astype(jnp.bfloat16)


def attention(q, k, v, far, w_key, w_value, bias, w_out, lifted):
    rows, width = q.shape
    block = 256
    return pl.pallas_call(
        attention_kernel,
        grid=(width // block,),
        in_specs=[LOCAL] * 9,
        out_specs=LOCAL,
        out_shape=jax.ShapeDtypeStruct((rows, width), jnp.bfloat16),
        scratch_shapes=[
            pltpu.VMEM((width // block, block, rows), jnp.bfloat16),
            pltpu.VMEM((far.shape[0], block), jnp.bfloat16),
            pltpu.VMEM((block, far.shape[0]), jnp.bfloat16),
        ],
        compiler_params=pltpu.CompilerParams(
            dimension_semantics=("arbitrary",), vmem_limit_bytes=28 << 20
        ),
        name="window_attention",
    )(q, k, v, far, w_key, w_value, bias, w_out, lifted)


def steps(
    image_tokens,
    lift_weight,
    route_token,
    route_cell,
    slot_counts,
    norm_gain,
    w_query,
    w_key,
    w_value,
    w_out,
    key_bias,
):
    n_y = lax.axis_size("bevy")
    n_x = lax.axis_size("bevx")
    slot_count = route_token.shape[3]
    width = lift_weight.shape[1]
    head_count = key_bias.shape[2]
    grid_rows = key_bias.shape[0]
    own_cells = ROWS_DEV * COLS_DEV
    edge = HALO * COLS_DEV
    ext = own_cells + edge
    row = lax.axis_index("bevy")
    col = lax.axis_index("bevx")
    core = lax.axis_index("cam")
    up = [(i, (i + 1) % n_x) for i in range(n_x)]
    down = [(b, a) for a, b in up]
    swap = [(0, 1), (1, 0)]
    at = jnp.stack([col, core * edge]).astype(jnp.int32)

    def shift(value, perm):
        return lax.ppermute(value, "bevx", perm)

    u1 = shift(image_tokens, up)
    d1 = shift(image_tokens, down)

    def by_column(value):
        return value.reshape(n_y, n_x, slot_count).transpose(1, 0, 2).reshape(n_x, -1)

    is_live = (
        lax.broadcasted_iota(jnp.int32, route_token.shape[2:], 1) < slot_counts[0, 0][:, None]
    )
    route = by_column(jnp.where(is_live, route_token[0, 0], -1))
    cells = by_column(route_cell[:, 0, 0, :])
    route, cells = lax.optimization_barrier((route, cells))
    cells_other = lax.ppermute(cells, "cam", swap)
    route = lax.all_to_all(route, "bevx", split_axis=0, concat_axis=0, tiled=True)

    u2 = shift(u1, up)
    d2 = shift(d1, down)
    u3 = shift(u2, up)
    d3 = shift(d2, down)
    low, high = cut(u3, d3)
    u4 = shift(low, up)
    d4 = shift(high, down)

    near_row = (row * 2 + core) * ROWS_DEV - core * HALO
    far_row = (row * 2 + core) * ROWS_DEV + jnp.where(core == 0, -HALO, ROWS_DEV)
    far_ok = (far_row >= 0) & (far_row < grid_rows)
    near_bias = lax.dynamic_slice_in_dim(key_bias, near_row, ROWS_DEV + HALO, 0)
    far_bias = lax.dynamic_slice_in_dim(
        key_bias, jnp.clip(far_row, 0, grid_rows - HALO), HALO, 0
    )
    far_bias = jnp.where(far_ok, far_bias, jnp.asarray(MASKED, jnp.bfloat16))
    bias = jnp.concatenate([near_bias, far_bias], axis=0).reshape(-1, head_count)
    bias = jnp.pad(bias, ((0, 0), (0, 1)), constant_values=1)
    bias = jnp.pad(bias, ((0, 0), (0, 127 - head_count)))

    def exchange(rows):
        got = lax.all_to_all(rows, "bevy", split_axis=0, concat_axis=0, tiled=True)
        return got, lax.ppermute(got, "cam", swap)

    rows = pick(EARLY, n_x, n_y, at, route, (image_tokens, u1, d1, u2, d2))
    rows, bias, cells_other = lax.optimization_barrier((rows, bias, cells_other))
    early, early_other = exchange(rows)
    total = jax.ShapeDtypeStruct((ext, width), jnp.float32)
    [lifted] = local_call(
        lambda *refs: first_sum_kernel(n_x, *refs), (at, early, cells, lift_weight), [total]
    )
    [lifted] = local_call(
        lambda *refs: second_sum_kernel(n_x, *refs),
        (at, lifted, early_other, cells_other, lift_weight),
        [total],
    )
    rows = pick(LATE, n_x, n_y, at, route, (u3, d3, u4, d4))
    late, late_other = exchange(rows)
    [lifted] = local_call(
        lambda *refs: next_sum_kernel(n_x, *refs),
        (
            at,
            pltpu.with_memory_space_constraint(lifted, pltpu.HBM),
            late,
            cells,
            lift_weight,
        ),
        [total],
        [pltpu.SemaphoreType.DMA],
        (1,),
    )
    own_lifted, normed, sent = local_call(
        lambda *refs: last_sum_kernel(n_x, edge, *refs),
        (at, lifted, late_other, cells_other, lift_weight, norm_gain.reshape(1, -1)),
        [
            jax.ShapeDtypeStruct((own_cells, width), jnp.float32),
            jax.ShapeDtypeStruct((ext, width), jnp.bfloat16),
            jax.ShapeDtypeStruct((edge, width), jnp.bfloat16),
        ],
        [pltpu.VMEM((ext, width), jnp.float32)],
    )
    hops = [(2 * i, 2 * i - 1) for i in range(1, n_y)] + [
        (2 * i + 1, 2 * i + 2) for i in range(n_y - 1)
    ]
    far = lax.ppermute(sent, ("bevy", "cam"), hops)
    queries, keys, values = project(at, normed, w_query, w_key, w_value, own_cells)

    out = attention(
        queries, keys, values, far, w_key, w_value, bias, w_out, own_lifted
    )
    return out.reshape(ROWS_DEV, COLS_DEV, width)


def solution(mesh):
    placed = (
        P(("bevy", "bevx", "cam"), None),
        P(),
        P(("bevy", "bevx"), "cam", None, None),
        P(None, "cam", ("bevy", "bevx"), None),
        P(("bevy", "bevx"), "cam", None),
        P(),
        P(),
        P(),
        P(),
        P(),
        P(None, "bevx", None),
    )
    return jax.shard_map(
        steps,
        mesh=mesh,
        in_specs=placed,
        out_specs=P(("bevy", "cam"), "bevx", None),
        check_vma=False,
    )
```
